128 devices in a mesh: dp: 8 (over y, core), mp: 16 (over x, z).
Axes of the slice: x: 4, y: 4, z: 4, core: 2. Of those that a mesh axis runs over, the one named last changes fastest.
Arguments:
- tokens: bfloat16 [1024, 8192], P('dp', 'mp'), may hold values from -6 to 6
- grad_out: bfloat16 [1024, 8192], P('dp', 'mp'), may hold values from -6 to 6
- gate_weight: bfloat16 [1024, 128, 128], P('mp'), may hold values from -0.1875 to 0.1875
- up_weight: bfloat16 [1024, 128, 128], P('mp'), may hold values from -0.1875 to 0.1875
- down_weight: bfloat16 [1024, 128, 128], P('mp'), may hold values from -0.125 to 0.125
- gate_block_pairs: int32 [1024, 2], replicated, may hold values from 0 to 111, as said below
- up_blocks: int32 [1024, 2], replicated, may hold values from 0 to 111, as said below
- down_blocks: int32 [1024, 2], replicated, may hold values from 0 to 111, as said below
- column_order: int32 [112], replicated, may hold values from 0 to 111, as said below
Outputs:
- hidden_owned: bfloat16 [1024, 14336], P('dp', 'mp')
- output: bfloat16 [1024, 8192], P('dp', 'mp')
- input_grad: bfloat16 [1024, 8192], P('dp', 'mp')
- gate_grad: bfloat16 [1024, 128, 128], P('mp', 'dp')
- up_grad: bfloat16 [1024, 128, 128], P('mp', 'dp')
- down_grad: bfloat16 [1024, 128, 128], P('mp', 'dp')
The draws below stay inside these ranges and needn't reach their ends.
Inputs may be any that keep to these rules, and one draw needn't show every extreme that they name: A permutation of the hidden column blocks; index j of mp owns the column blocks column_order[j * 7] to column_order[(j + 1) * 7 - 1]. `gate_block_pairs`: row k holds the row block (of 64) and column block (of 112) of gate block k; no block appears twice; block k = i * 64 + j * 4 + s with 0 <= s < 4 lies in a column block owned by index j; every column block holds at least one block. `up_blocks`: as gate_block_pairs, for the up blocks. `down_blocks`: row k holds the hidden block (of 112) and width block (of 64) of down block k; no block appears twice; block k = i * 64 + j * 4 + s with 0 <= s < 4 lies in a hidden block owned by index j; every hidden block holds at least one block.
All inputs are finite; a program needn't handle non-finite values.
Results may differ from the reference program's by a relative error of at most 0.024.
Values may be sent and summed in bfloat16 or wider, within the bound.
No kernel may reach another device: no remote copies, remote signals or barrier semaphores. Data moves between devices by JAX's collectives and lax.ppermute only.
A program may use at most 128 MiB of HBM per device.

```python
import jax
import jax.numpy as jnp
from jax import lax

D = 8192
FF = 14336
BS = 128
TOK_DEV = 128
BLK_DEV = 64
TOKENS = 1024
RB = 64
CB = 112
NB = 1024
N_DP = 8
N_MP = 16


def owner_columns(key):
    return jax.random.permutation(jax.random.fold_in(key, 7), CB).astype(jnp.int32)


def draw_column_order(key, part):
    return owner_columns(key)


def owner_cells(key, salt):
    order = owner_columns(key)
    owned = CB // N_MP
    cells = owned * RB
    quota = BLK_DEV // N_MP
    cell_ids = jnp.arange(cells, dtype=jnp.int32)
    column_within = cell_ids % owned
    row_of_cell = cell_ids // owned

    def one_owner(owner):
        owner_key = jax.random.fold_in(jax.random.fold_in(key, salt), owner)
        offset_start = jax.random.randint(jax.random.fold_in(owner_key, 1), (cells,), 0, 2 ** 19, dtype=jnp.int32) * cells + cell_ids
        selected_rows = jax.random.randint(jax.random.fold_in(owner_key, 2), (owned,), 0, RB, dtype=jnp.int32)
        extra_reward = row_of_cell == jnp.take(selected_rows, column_within)
        ranking_values = offset_start + jnp.where(extra_reward, 2 ** 30, 0).astype(jnp.int32)
        chosen = lax.top_k(ranking_values, BLK_DEV)[1].astype(jnp.int32)
        columns = jnp.take(order, owner * owned + chosen % owned)
        return ((chosen // owned).astype(jnp.int32), columns.astype(jnp.int32))
    rows, columns = jax.vmap(one_owner)(jnp.arange(N_MP, dtype=jnp.int32))
    rows = rows.reshape(N_MP, N_MP, quota).transpose(1, 0, 2).reshape(-1)
    columns = columns.reshape(N_MP, N_MP, quota).transpose(1, 0, 2).reshape(-1)
    return (rows, columns)


def draw_gate_block_pairs(key, part):
    rows, columns = owner_cells(key, 101)
    return jnp.stack([rows, columns], axis=1).astype(jnp.int32)


def draw_up_blocks(key, part):
    rows, columns = owner_cells(key, 202)
    return jnp.stack([rows, columns], axis=1).astype(jnp.int32)


def draw_down_blocks(key, part):
    rows, columns = owner_cells(key, 303)
    return jnp.stack([columns, rows], axis=1).astype(jnp.int32)


def shard_levels(key, extent, shards, low, top_value):
    gain = 1.0
    for position, parts in shards:
        steps = jax.random.uniform(jax.random.fold_in(jax.random.fold_in(key, 6), position), (parts,), jnp.float32, low / len(shards), top_value / len(shards))
        gain = gain * jnp.repeat(jnp.exp(steps), extent[position] // parts).reshape((-1,) + (1,) * (len(extent) - 1 - position))
    return gain


def centred(key, extent, scale, limit, shards=(), kind=jnp.bfloat16):
    values = jax.random.normal(key, extent, jnp.float32) * scale
    if len(shards) > 0:
        values = shard_levels(key, extent, shards, -0.22, 0.18) * values
    return jnp.clip(values, min=-limit, max=limit).astype(kind)


def setup_inputs(seed: int = 0) -> dict:
    splits = jax.random.split(jax.random.key(seed), 10)
    return {
        "tokens": centred(splits[0], (TOKENS, D), 1.0, 6.0, ((0, 8), (1, 16))),
        "grad_out": centred(splits[1], (TOKENS, D), 1.0, 6.0, ((0, 8), (1, 16))),
        "gate_weight": centred(splits[2], (NB, BS, BS), (NB * BS // CB) ** -0.5, 0.1875, ((0, 16),)),
        "up_weight": centred(splits[3], (NB, BS, BS), (NB * BS // CB) ** -0.5, 0.1875, ((0, 16),)),
        "down_weight": centred(splits[4], (NB, BS, BS), (NB * BS // RB) ** -0.5, 0.125, ((0, 16),)),
        "gate_block_pairs": draw_gate_block_pairs(jax.random.fold_in(splits[9], 71), 0),
        "up_blocks": draw_up_blocks(jax.random.fold_in(splits[9], 71), 0),
        "down_blocks": draw_down_blocks(jax.random.fold_in(splits[9], 71), 0),
        "column_order": draw_column_order(jax.random.fold_in(splits[9], 71), 0),
    }


def to_blocks(matrix, block_size):
    return matrix.reshape(matrix.shape[0], matrix.shape[1] // block_size, block_size).transpose(1, 0, 2)


def from_blocks(blocks):
    return blocks.transpose(1, 0, 2).reshape(blocks.shape[1], blocks.shape[0] * blocks.shape[2])


def rounded(values):
    return lax.optimization_barrier(values.astype(jnp.bfloat16)).astype(jnp.float32)


def silu_parts(gate_sum):
    sigmoid = jax.nn.sigmoid(gate_sum)
    return gate_sum * sigmoid, sigmoid


def device_sums(block_sets, segment_count, einsum_form, round_shares):
    sources = [block_set[0] for block_set in block_sets]
    stacked = tuple((block_set[1].reshape(N_MP, -1), block_set[2].reshape(N_MP, -1), block_set[3].reshape((N_MP, -1) + block_set[3].shape[1:])) for block_set in block_sets)
    initial = jnp.zeros((segment_count, sources[0].shape[1], sources[0].shape[2]), jnp.float32)

    def add_device(running, pieces):
        device_term = jnp.zeros_like(running)
        for source, members in zip(sources, pieces):
            gathered = jnp.take(source, members[0], axis=0).astype(jnp.float32)
            product = jnp.einsum(einsum_form, gathered, members[2].astype(jnp.float32))
            device_term = device_term + jax.ops.segment_sum(product, members[1], num_segments=segment_count)
        if round_shares:
            device_term = rounded(device_term)
        return running + device_term, None

    result = lax.scan(add_device, initial, stacked)
    return result[0]


def grouped(blocks):
    return blocks.reshape(blocks.shape[0], N_DP, TOK_DEV, blocks.shape[2]).transpose(1, 0, 2, 3)


def weight_grads(grad_sets):
    indices = [(grad_set[1], grad_set[3]) for grad_set in grad_sets]
    group_data = tuple((grouped(grad_set[0]), grouped(grad_set[2])) for grad_set in grad_sets)
    initial = tuple(jnp.zeros((grad_set[1].shape[0], BS, BS), jnp.float32) for grad_set in grad_sets)

    def add_group(running, groups):
        updated = []
        for current, members, index_pair in zip(running, groups, indices):
            left_rows = jnp.take(members[0], index_pair[0], axis=0).astype(jnp.float32)
            right_rows = jnp.take(members[1], index_pair[1], axis=0).astype(jnp.float32)
            updated.append(current + rounded(jnp.einsum("btk,btn->bkn", left_rows, right_rows)))
        return tuple(updated), None

    result = lax.scan(add_group, initial, group_data)
    return tuple(current.astype(jnp.bfloat16) for current in result[0])


def reference(tokens, grad_out, gate_weight, up_weight, down_weight, gate_block_pairs, up_blocks, down_blocks, column_order):
    inputs = to_blocks(tokens, BS)
    cotangent = to_blocks(grad_out, BS)
    gate_sum = device_sums(((inputs, gate_block_pairs[:, 0], gate_block_pairs[:, 1], gate_weight),), FF // BS, "btk,bkn->btn", True)
    up_sum = device_sums(((inputs, up_blocks[:, 0], up_blocks[:, 1], up_weight),), FF // BS, "btk,bkn->btn", True)
    activated, sigmoid = silu_parts(gate_sum)
    hidden = (activated * up_sum).astype(jnp.bfloat16)
    output = device_sums(((hidden, down_blocks[:, 0], down_blocks[:, 1], down_weight),), D // BS, "btk,bkn->btn", False).astype(jnp.bfloat16)
    hidden_grad = device_sums(((cotangent, down_blocks[:, 1], down_blocks[:, 0], down_weight),), FF // BS, "btn,bkn->btk", True)
    gate_delta = (hidden_grad * up_sum * sigmoid * (1.0 + gate_sum * (1.0 - sigmoid))).astype(jnp.bfloat16)
    up_delta = (hidden_grad * activated).astype(jnp.bfloat16)
    input_grad = device_sums(((gate_delta, gate_block_pairs[:, 1], gate_block_pairs[:, 0], gate_weight), (up_delta, up_blocks[:, 1], up_blocks[:, 0], up_weight)), D // BS, "btn,bkn->btk", False).astype(jnp.bfloat16)
    grads = weight_grads(((inputs, gate_block_pairs[:, 0], gate_delta, gate_block_pairs[:, 1]), (inputs, up_blocks[:, 0], up_delta, up_blocks[:, 1]), (hidden, down_blocks[:, 0], cotangent, down_blocks[:, 1])))
    hidden_owned = from_blocks(jnp.take(hidden, column_order, axis=0))
    return hidden_owned, from_blocks(output), from_blocks(input_grad), grads[0], grads[1], grads[2]
```

```python
import functools

import jax
import jax.numpy as jnp
from jax import lax
from jax.experimental import pallas as pl
from jax.experimental.pallas import tpu as pltpu
from jax.sharding import PartitionSpec as P

BS = 128
STEPS = 8
BF = jnp.bfloat16
F32 = jnp.float32


def dot(a, b):
    return lax.dot_general(a, b, (((1,), (0,)), ((), ())), preferred_element_type=F32)


def dot_t(a, b):
    return lax.dot_general(a, b, (((1,), (1,)), ((), ())), preferred_element_type=F32)


def wide(ref, which, block, per):
    lane = pl.multiple_of((block % per) * BS, BS)
    return ref[block // per, which, :, pl.ds(lane, BS)]


def sums_kernel(rows, cols, x_ref, w_ref, act_ref, own_ref, acc, *, per, quota, owned):
    step = pl.program_id(0)
    group = w_ref.shape[1]

    @pl.when(step == 0)
    def _():
        acc[...] = jnp.zeros_like(acc)

    for b in range(group):
        proj = (b // quota) % 3
        r = rows[step * group + b]
        c = cols[step * group + b]
        w = w_ref[:, b].reshape(BS, BS)
        if proj < 2:
            acc[proj, c] += dot(wide(x_ref, 0, r, per), w)
        else:
            acc[proj, c] += dot_t(wide(x_ref, 1, r, per), w)

    @pl.when(step == pl.num_programs(0) - 1)
    def _():
        for c in range(owned):
            gate, up, grad = acc[0, c], acc[1, c], acc[2, c]
            s = jax.nn.sigmoid(gate)
            silu = gate * s
            hidden = (silu * up).astype(BF)
            act_ref[0, c] = hidden
            own_ref[:, c * BS : (c + 1) * BS] = hidden
            act_ref[1, c] = (grad * up * s * (1.0 + gate * (1.0 - s))).astype(BF)
            act_ref[2, c] = (grad * silu).astype(BF)


def parts_kernel(rows, cols, act_ref, w_ref, out_ref, acc, *, per, quota):
    step = pl.program_id(0)
    group = w_ref.shape[1]

    @pl.when(step == 0)
    def _():
        acc[...] = jnp.zeros_like(acc)

    for b in range(group):
        proj = (b // quota) % 3
        r = rows[step * group + b]
        c = cols[step * group + b]
        w = w_ref[:, b].reshape(BS, BS)
        if proj < 2:
            acc[1, r] += dot_t(act_ref[1 + proj, c], w)
        else:
            acc[0, r] += dot(act_ref[0, c], w)

    @pl.when(step == pl.num_programs(0) - 1)
    def _():
        def store(dest, carry):
            for which in range(2):
                for q in range(per):
                    out_ref[dest, which, :, q * BS : (q + 1) * BS] = acc[
                        which, dest * per + q
                    ].astype(BF)
            return carry

        lax.fori_loop(0, out_ref.shape[0], store, 0)


def grads_kernel(rows, cols, xt_ref, x_ref, act_ref, out_ref, ht, *, per, quota):
    step = pl.program_id(0)
    group = out_ref.shape[1]

    @pl.when(step == 0)
    def _():
        for c in range(ht.shape[0]):
            ht[c] = act_ref[0, c].T

    for b in range(group):
        proj = (b // quota) % 3
        r = rows[step * group + b]
        c = cols[step * group + b]
        if proj < 2:
            g = dot(xt_ref[r], act_ref[1 + proj, c])
        else:
            g = dot(ht[c], wide(x_ref, 1, r, per))
        out_ref[:, b] = g.astype(BF).reshape(out_ref.shape[0], -1, BS)


def flip_kernel(x_ref, out_ref, *, per):
    for q in range(per):
        out_ref[q] = x_ref[0, 0, :, q * BS : (q + 1) * BS].T


def full(shape):
    return pl.BlockSpec(shape, lambda *a: (0,) * len(shape))


def body(
    tokens,
    grad_out,
    gate_weight,
    up_weight,
    down_weight,
    gate_block_pairs,
    up_blocks,
    down_blocks,
    column_order,
):
    n_mp, n_dp = lax.axis_size("mp"), lax.axis_size("dp")
    member, shard = lax.axis_index("mp"), lax.axis_index("dp")
    held = gate_weight.shape[0]
    quota = held // n_mp
    slab = BS // n_dp
    per = tokens.shape[1] // BS
    n_rows = per * n_mp
    owned = column_order.shape[0] // n_mp
    total = 3 * held
    group = total // STEPS
    tok = tokens.shape[0]

    x_all = lax.all_gather(jnp.stack([tokens, grad_out]), "mp", axis=0, tiled=False)

    slabs = jnp.stack(
        [
            lax.dynamic_slice_in_dim(w, shard * slab, slab, 1).reshape(n_mp, quota, slab, BS)
            for w in (gate_weight, up_weight, down_weight)
        ],
        axis=1,
    )
    mine = lax.all_to_all(slabs, "mp", split_axis=0, concat_axis=0, tiled=True)
    weights = lax.all_gather(mine.reshape(total, slab, BS), "dp", axis=0, tiled=False)

    tables = jnp.stack([gate_block_pairs, up_blocks, down_blocks[:, ::-1]])
    tables = tables.reshape(3, n_mp, n_mp, quota, 2)
    tables = lax.dynamic_index_in_dim(tables, member, 2, keepdims=False)
    tables = tables.transpose(1, 0, 2, 3).reshape(total, 2)
    own_cols = lax.dynamic_slice_in_dim(column_order, member * owned, owned, 0)
    rows = tables[:, 0]
    cols = jnp.sum(
        jnp.where(
            tables[:, 1][:, None] == own_cols[None, :], jnp.arange(owned, dtype=jnp.int32), 0
        ),
        axis=1,
    )

    x_spec = full(x_all.shape)
    w_spec = pl.BlockSpec((n_dp, group, slab, BS), lambda g, *_: (0, g, 0, 0))
    act_shape = (3, owned, tok, BS)
    params = pltpu.CompilerParams(dimension_semantics=("arbitrary",))

    x_t = pl.pallas_call(
        functools.partial(flip_kernel, per=per),
        out_shape=jax.ShapeDtypeStruct((n_rows, BS, tok), BF),
        grid=(n_mp,),
        in_specs=[pl.BlockSpec((1, 1, tok, per * BS), lambda g: (g, 0, 0, 0))],
        out_specs=pl.BlockSpec((per, BS, tok), lambda g: (g, 0, 0)),
        compiler_params=params,
        name="flip",
    )(x_all)

    act, hidden_own = pl.pallas_call(
        functools.partial(sums_kernel, per=per, quota=quota, owned=owned),
        out_shape=(
            jax.ShapeDtypeStruct(act_shape, BF),
            jax.ShapeDtypeStruct((tok, owned * BS), BF),
        ),
        grid_spec=pltpu.PrefetchScalarGridSpec(
            num_scalar_prefetch=2,
            grid=(STEPS,),
            in_specs=[x_spec, w_spec],
            out_specs=[full(act_shape), full((tok, owned * BS))],
            scratch_shapes=[pltpu.VMEM(act_shape, F32)],
        ),
        compiler_params=params,
        name="sums",
    )(rows, cols, x_all, weights)

    grads = pl.pallas_call(
        functools.partial(grads_kernel, per=per, quota=quota),
        out_shape=jax.ShapeDtypeStruct((n_dp, total, slab, BS), BF),
        grid_spec=pltpu.PrefetchScalarGridSpec(
            num_scalar_prefetch=2,
            grid=(STEPS,),
            in_specs=[full(x_t.shape), x_spec, full(act_shape)],
            out_specs=w_spec,
            scratch_shapes=[pltpu.VMEM((owned, BS, tok), BF)],
        ),
        compiler_params=params,
        name="grads",
    )(rows, cols, x_t, x_all, act)
    grads = lax.psum_scatter(grads, "dp", scatter_dimension=0, tiled=True)

    parts = pl.pallas_call(
        functools.partial(parts_kernel, per=per, quota=quota),
        out_shape=jax.ShapeDtypeStruct((n_mp, 2, tok, per * BS), BF),
        grid_spec=pltpu.PrefetchScalarGridSpec(
            num_scalar_prefetch=2,
            grid=(STEPS,),
            in_specs=[full(act_shape), w_spec],
            out_specs=full((n_mp, 2, tok, per * BS)),
            scratch_shapes=[pltpu.VMEM((2, n_rows, tok, BS), F32)],
        ),
        compiler_params=params,
        name="parts",
    )(rows, cols, act, weights)
    parts = lax.all_to_all(parts, "mp", split_axis=0, concat_axis=0, tiled=True)
    output = jnp.sum(parts[:, 0].astype(F32), axis=0).astype(BF)
    input_grad = jnp.sum(parts[:, 1].astype(F32), axis=0).astype(BF)

    grads = grads.reshape(n_mp, 3, quota, slab, BS)
    grads = lax.all_to_all(grads, "mp", split_axis=0, concat_axis=0, tiled=True)
    gate_grad, up_grad, down_grad = (
        grads[:, p].reshape(held, slab, BS) for p in range(3)
    )
    return (hidden_own, output, input_grad, gate_grad, up_grad, down_grad)


def solution(mesh):
    return jax.shard_map(
        body,
        mesh=mesh,
        in_specs=(
            P("dp", "mp"),
            P("dp", "mp"),
            P("mp", None, None),
            P("mp", None, None),
            P("mp", None, None),
            P(),
            P(),
            P(),
            P(),
        ),
        out_specs=(
            P("dp", "mp"),
            P("dp", "mp"),
            P("dp", "mp"),
            P("mp", "dp", None),
            P("mp", "dp", None),
            P("mp", "dp", None),
        ),
        check_vma=False,
    )
```

```python
import functools

import jax
import jax.numpy as jnp
from jax import lax
from jax.experimental import pallas as pl
from jax.experimental.pallas import tpu as pltpu
from jax.sharding import Mesh, PartitionSpec as P

BS = 128
STEPS = 8
MP = ("x", "z")
DP = ("y", "c")
BF = jnp.bfloat16
F32 = jnp.float32


def dot(a, b):
    return lax.dot_general(a, b, (((1,), (0,)), ((), ())), preferred_element_type=F32)


def dot_t(a, b):
    return lax.dot_general(a, b, (((1,), (1,)), ((), ())), preferred_element_type=F32)


def wide(ref, which, block, per):
    lane = pl.multiple_of((block % per) * BS, BS)
    return ref[block // per, which, :, pl.ds(lane, BS)]


def sums_kernel(rows, cols, x_ref, w_ref, act_ref, own_ref, acc, *, per, quota, owned):
    step = pl.program_id(0)
    group = w_ref.shape[1]

    @pl.when(step == 0)
    def _():
        acc[...] = jnp.zeros_like(acc)

    for b in range(group):
        proj = (b // quota) % 3
        r = rows[step * group + b]
        c = cols[step * group + b]
        w = w_ref[:, b].reshape(BS, BS)
        if proj < 2:
            acc[proj, c] += dot(wide(x_ref, 0, r, per), w)
        else:
            acc[proj, c] += dot_t(wide(x_ref, 1, r, per), w)

    @pl.when(step == pl.num_programs(0) - 1)
    def _():
        for c in range(owned):
            gate, up, grad = acc[0, c], acc[1, c], acc[2, c]
            s = jax.nn.sigmoid(gate)
            silu = gate * s
            hidden = (silu * up).astype(BF)
            act_ref[0, c] = hidden
            own_ref[:, c * BS : (c + 1) * BS] = hidden
            act_ref[1, c] = (grad * up * s * (1.0 + gate * (1.0 - s))).astype(BF)
            act_ref[2, c] = (grad * silu).astype(BF)


def parts_kernel(rows, cols, place, act_ref, w_ref, *refs, per, quota):
    outs, acc = refs[:-1], refs[-1]
    ring = len(outs) // 2
    step = pl.program_id(0)
    group = w_ref.shape[1]

    @pl.when(step == 0)
    def _():
        acc[...] = jnp.zeros_like(acc)

    for b in range(group):
        proj = (b // quota) % 3
        r = rows[step * group + b]
        c = cols[step * group + b]
        w = w_ref[:, b].reshape(BS, BS)
        if proj < 2:
            acc[1, r] += dot_t(act_ref[1 + proj, c], w)
        else:
            acc[0, r] += dot(act_ref[0, c], w)

    @pl.when(step == pl.num_programs(0) - 1)
    def _():
        for hop in range(ring):
            for turn in range(ring):
                near = (place[0] + hop) % ring, (place[1] + hop) % ring
                far = (place[0] + turn) % ring, (place[1] + turn) % ring
                dests = near[0] * ring + far[1], far[0] * ring + near[1]
                for which in range(2):
                    for q in range(per):
                        outs[which * ring + hop][turn, :, q * BS : (q + 1) * BS] = acc[
                            which, dests[which] * per + q
                        ].astype(BF)


def grads_kernel(rows, cols, xt_ref, x_ref, act_ref, out_ref, ht, *, per, quota):
    step = pl.program_id(0)
    group = out_ref.shape[1]

    @pl.when(step == 0)
    def _():
        for c in range(ht.shape[0]):
            ht[c] = act_ref[0, c].T

    for b in range(group):
        proj = (b // quota) % 3
        r = rows[step * group + b]
        c = cols[step * group + b]
        if proj < 2:
            g = dot(xt_ref[r], act_ref[1 + proj, c])
        else:
            g = dot(ht[c], wide(x_ref, 1, r, per))
        out_ref[:, b] = g.astype(BF).reshape(out_ref.shape[0], -1, BS)


def flip_kernel(x_ref, out_ref, *, per):
    for q in range(per):
        out_ref[q] = x_ref[0, 0, :, q * BS : (q + 1) * BS].T


def shift(value, axis, hop):
    size = lax.axis_size(axis)
    return lax.ppermute(value, axis, [(i, (i + hop) % size) for i in range(size)])


def spread(mine, n_dp):
    ring = lax.axis_size("y")
    y, core = lax.axis_index("y"), lax.axis_index("c")
    half = mine.shape[0] // 2
    up, down = shift(mine, "y", 1), shift(mine, "y", -1)
    lo, hi = shift(up[:half], "y", 1), shift(down[half:], "y", -1)
    whole = jnp.zeros((n_dp,) + mine.shape, mine.dtype)
    for value, hop, start in ((mine, 0, 0), (up, -1, 0), (down, 1, 0), (lo, 2, 0), (hi, 2, half)):
        place = (y + hop) % ring * 2
        other = shift(value, "c", 1)
        whole = lax.dynamic_update_slice(whole, value[None], (place + core, start, 0, 0))
        whole = lax.dynamic_update_slice(whole, other[None], (place + 1 - core, start, 0, 0))
    return whole


def collect(outs, grads):
    ring = len(outs)
    total = lambda terms: sum(t.astype(F32) for t in terms)
    first = [[p[0]] + [shift(p[h], a, h) for h in range(1, ring)] for p, a in ((outs, "x"), (grads, "z"))]
    done = []
    for terms, axis in zip(first, ("z", "x")):
        sums = [total([t[turn] for t in terms]) for turn in range(ring)]
        arrived = [shift(sums[turn].astype(BF), axis, turn) for turn in range(1, ring)]
        done.append(total([sums[0]] + arrived).astype(BF))
    return done


def full(shape):
    return pl.BlockSpec(shape, lambda *a: (0,) * len(shape))


def body(
    tokens,
    grad_out,
    gate_weight,
    up_weight,
    down_weight,
    gate_block_pairs,
    up_blocks,
    down_blocks,
    column_order,
):
    n_mp, n_dp = lax.axis_size(MP), lax.axis_size(DP)
    member, shard = lax.axis_index(MP), lax.axis_index(DP)
    ring = lax.axis_size("x")
    held = gate_weight.shape[0]
    quota = held // n_mp
    slab = BS // n_dp
    per = tokens.shape[1] // BS
    n_rows = per * n_mp
    owned = column_order.shape[0] // n_mp
    total = 3 * held
    group = total // STEPS
    tok = tokens.shape[0]

    x_all = lax.all_gather(jnp.stack([tokens, grad_out]), MP, axis=0, tiled=False)

    slabs = jnp.stack(
        [
            lax.dynamic_slice_in_dim(w, shard * slab, slab, 1).reshape(n_mp, quota, slab, BS)
            for w in (gate_weight, up_weight, down_weight)
        ],
        axis=1,
    )
    mine = lax.all_to_all(slabs, MP, split_axis=0, concat_axis=0, tiled=True)
    weights = spread(mine.reshape(total, slab, BS), n_dp)

    tables = jnp.stack([gate_block_pairs, up_blocks, down_blocks[:, ::-1]])
    tables = tables.reshape(3, n_mp, n_mp, quota, 2)
    tables = lax.dynamic_index_in_dim(tables, member, 2, keepdims=False)
    tables = tables.transpose(1, 0, 2, 3).reshape(total, 2)
    own_cols = lax.dynamic_slice_in_dim(column_order, member * owned, owned, 0)
    rows = tables[:, 0]
    cols = jnp.sum(
        jnp.where(
            tables[:, 1][:, None] == own_cols[None, :], jnp.arange(owned, dtype=jnp.int32), 0
        ),
        axis=1,
    )

    x_spec = full(x_all.shape)
    w_spec = pl.BlockSpec((n_dp, group, slab, BS), lambda g, *_: (0, g, 0, 0))
    act_shape = (3, owned, tok, BS)
    params = pltpu.CompilerParams(dimension_semantics=("arbitrary",))

    x_t = pl.pallas_call(
        functools.partial(flip_kernel, per=per),
        out_shape=jax.ShapeDtypeStruct((n_rows, BS, tok), BF),
        grid=(n_mp,),
        in_specs=[pl.BlockSpec((1, 1, tok, per * BS), lambda g: (g, 0, 0, 0))],
        out_specs=pl.BlockSpec((per, BS, tok), lambda g: (g, 0, 0)),
        compiler_params=params,
        name="flip",
    )(x_all)

    act, hidden_own = pl.pallas_call(
        functools.partial(sums_kernel, per=per, quota=quota, owned=owned),
        out_shape=(
            jax.ShapeDtypeStruct(act_shape, BF),
            jax.ShapeDtypeStruct((tok, owned * BS), BF),
        ),
        grid_spec=pltpu.PrefetchScalarGridSpec(
            num_scalar_prefetch=2,
            grid=(STEPS,),
            in_specs=[x_spec, w_spec],
            out_specs=[full(act_shape), full((tok, owned * BS))],
            scratch_shapes=[pltpu.VMEM(act_shape, F32)],
        ),
        compiler_params=params,
        name="sums",
    )(rows, cols, x_all, weights)

    grads = pl.pallas_call(
        functools.partial(grads_kernel, per=per, quota=quota),
        out_shape=jax.ShapeDtypeStruct((n_dp, total, slab, BS), BF),
        grid_spec=pltpu.PrefetchScalarGridSpec(
            num_scalar_prefetch=2,
            grid=(STEPS,),
            in_specs=[full(x_t.shape), x_spec, full(act_shape)],
            out_specs=w_spec,
            scratch_shapes=[pltpu.VMEM((owned, BS, tok), BF)],
        ),
        compiler_params=params,
        name="grads",
    )(rows, cols, x_t, x_all, act)
    grads = lax.psum_scatter(grads, DP, scatter_dimension=0, tiled=True)

    place = jnp.stack([lax.axis_index("x"), lax.axis_index("z")]).astype(jnp.int32)
    part_shape = (ring, tok, per * BS)
    parts = pl.pallas_call(
        functools.partial(parts_kernel, per=per, quota=quota),
        out_shape=[jax.ShapeDtypeStruct(part_shape, BF)] * (2 * ring),
        grid_spec=pltpu.PrefetchScalarGridSpec(
            num_scalar_prefetch=3,
            grid=(STEPS,),
            in_specs=[full(act_shape), w_spec],
            out_specs=[full(part_shape)] * (2 * ring),
            scratch_shapes=[pltpu.VMEM((2, n_rows, tok, BS), F32)],
        ),
        compiler_params=params,
        name="parts",
    )(rows, cols, place, act, weights)
    output, input_grad = collect(parts[:ring], parts[ring:])

    grads = grads.reshape(n_mp, 3, quota, slab, BS)
    grads = lax.all_to_all(grads, MP, split_axis=0, concat_axis=0, tiled=True)
    gate_grad, up_grad, down_grad = (
        grads[:, p].reshape(held, slab, BS) for p in range(3)
    )
    return (hidden_own, output, input_grad, gate_grad, up_grad, down_grad)


def solution(mesh):
    mesh = Mesh(mesh.devices.reshape(4, 2, 4, 4), DP + MP)
    wide_spec, block_spec, grad_spec = P(DP, MP), P(MP, None, None), P(MP, DP, None)
    return jax.shard_map(
        body,
        mesh=mesh,
        in_specs=(wide_spec,) * 2 + (block_spec,) * 3 + (P(),) * 4,
        out_specs=(wide_spec,) * 3 + (grad_spec,) * 3,
        check_vma=False,
    )
```

```python
import functools

import jax
import jax.numpy as jnp
from jax import lax
from jax.experimental import pallas as pl
from jax.experimental.pallas import tpu as pltpu
from jax.sharding import Mesh, PartitionSpec as P

BS = 128
STEPS = 8
MP = ("x", "z")
DP = ("y", "c")
BF = jnp.bfloat16
F32 = jnp.float32


def dot(a, b):
    return lax.dot_general(a, b, (((1,), (0,)), ((), ())), preferred_element_type=F32)


def dot_t(a, b):
    return lax.dot_general(a, b, (((1,), (1,)), ((), ())), preferred_element_type=F32)


def wide(ref, which, block, per):
    lane = pl.multiple_of((block % per) * BS, BS)
    return ref[block // per, which, :, pl.ds(lane, BS)]


def assemble(slots, refs, whole):
    step = pl.program_id(0)
    early = step < pl.num_programs(0) // 2
    for i in range(2):
        whole[:, slots[i]] = refs[i][...]
    for half in range(2):

        @pl.when(early if half == 0 else jnp.logical_not(early))
        def _():
            for i in range(2, 8):
                whole[:, slots[i]] = refs[2 + 2 * (i - 2) + half][...]


def sums_kernel(rows, cols, slots, x_ref, *refs, per, quota, owned):
    pieces, (act_ref, own_ref, acc, whole) = refs[:-4], refs[-4:]
    step = pl.program_id(0)
    group = whole.shape[0]
    assemble(slots, pieces, whole)

    @pl.when(step == 0)
    def _():
        acc[...] = jnp.zeros_like(acc)

    for b in range(group):
        proj = (b // quota) % 3
        r = rows[step * group + b]
        c = cols[step * group + b]
        w = whole[b].reshape(BS, BS)
        if proj < 2:
            acc[proj, c] += dot(wide(x_ref, 0, r, per), w)
        else:
            acc[proj, c] += dot_t(wide(x_ref, 1, r, per), w)

    @pl.when(step == pl.num_programs(0) - 1)
    def _():
        for c in range(owned):
            gate, up, grad = acc[0, c], acc[1, c], acc[2, c]
            s = jax.nn.sigmoid(gate)
            silu = gate * s
            hidden = (silu * up).astype(BF)
            act_ref[0, c] = hidden
            own_ref[:, c * BS : (c + 1) * BS] = hidden
            act_ref[1, c] = (grad * up * s * (1.0 + gate * (1.0 - s))).astype(BF)
            act_ref[2, c] = (grad * silu).astype(BF)


def parts_kernel(rows, cols, slots, place, act_ref, *refs, per, quota, count):
    pieces, outs, (acc, whole) = refs[:count], refs[count:-2], refs[-2:]
    ring = len(outs) // 2
    step = pl.program_id(0)
    group = whole.shape[0]
    assemble(slots, pieces, whole)

    @pl.when(step == 0)
    def _():
        acc[...] = jnp.zeros_like(acc)

    for b in range(group):
        proj = (b // quota) % 3
        r = rows[step * group + b]
        c = cols[step * group + b]
        w = whole[b].reshape(BS, BS)
        if proj < 2:
            acc[1, r] += dot_t(act_ref[1 + proj, c], w)
        else:
            acc[0, r] += dot(act_ref[0, c], w)

    @pl.when(step == pl.num_programs(0) - 1)
    def _():
        for hop in range(ring):
            for turn in range(ring):
                near = (place[0] + hop) % ring, (place[1] + hop) % ring
                far = (place[0] + turn) % ring, (place[1] + turn) % ring
                dests = near[0] * ring + far[1], far[0] * ring + near[1]
                for which in range(2):
                    for q in range(per):
                        outs[which * ring + hop][turn, :, q * BS : (q + 1) * BS] = acc[
                            which, dests[which] * per + q
                        ].astype(BF)


def grads_kernel(rows, cols, xt_ref, x_ref, act_ref, out_ref, ht, *, per, quota):
    step = pl.program_id(0)
    group = out_ref.shape[1]

    @pl.when(step == 0)
    def _():
        for c in range(ht.shape[0]):
            ht[c] = act_ref[0, c].T

    for b in range(group):
        proj = (b // quota) % 3
        r = rows[step * group + b]
        c = cols[step * group + b]
        if proj < 2:
            g = dot(xt_ref[r], act_ref[1 + proj, c])
        else:
            g = dot(ht[c], wide(x_ref, 1, r, per))
        out_ref[:, b] = g.astype(BF).reshape(out_ref.shape[0], -1, BS)


def flip_kernel(x_ref, out_ref, *, per):
    index = lambda d: lax.broadcasted_iota(jnp.int32, (BS, BS), d)
    unit = jnp.where(index(0) == index(1), 1.0, 0.0).astype(BF)
    for j in range(x_ref.shape[0]):
        for q in range(per):
            x = x_ref[j, 0, :, q * BS : (q + 1) * BS]
            out_ref[j * per + q] = dot_t(unit, x).astype(BF)


def shift(value, axis, hop):
    size = lax.axis_size(axis)
    return lax.ppermute(value, axis, [(i, (i + hop) % size) for i in range(size)])


def spread(mine):
    half = mine.shape[0] // 2
    parts = mine[:half], mine[half:]
    up, down = [None] * 2, [None] * 2
    up[0], down[1] = shift(parts[0], "y", 1), shift(parts[1], "y", -1)
    up[1], down[0] = shift(parts[1], "y", 1), shift(parts[0], "y", -1)
    far = [shift(up[0], "y", 1), shift(down[1], "y", -1)]
    swap = lambda value: shift(value, "c", 1)
    pieces = [mine, swap(mine)]
    for pair in (up, down, far):
        pieces += pair + [swap(v) for v in pair]
    return pieces


def slots_of():
    ring, y, core = lax.axis_size("y"), lax.axis_index("y"), lax.axis_index("c")
    return jnp.stack([(y + hop + ring) % ring * 2 + c for hop in (0, -1, 1, 2) for c in (core, 1 - core)])


def collect(outs, grads):
    ring = len(outs)
    total = lambda terms: sum(t.astype(F32) for t in terms)
    first = [[p[0]] + [shift(p[h], a, h) for h in range(1, ring)] for p, a in ((outs, "x"), (grads, "z"))]
    done = []
    for terms, axis in zip(first, ("z", "x")):
        sums = [total([t[turn] for t in terms]) for turn in range(ring)]
        arrived = [shift(sums[turn].astype(BF), axis, turn) for turn in range(1, ring)]
        done.append(total([sums[0]] + arrived).astype(BF))
    return done


def full(shape):
    return pl.BlockSpec(shape, lambda *a: (0,) * len(shape))


def body(
    tokens,
    grad_out,
    gate_weight,
    up_weight,
    down_weight,
    gate_block_pairs,
    up_blocks,
    down_blocks,
    column_order,
):
    n_mp, n_dp = lax.axis_size(MP), lax.axis_size(DP)
    member, shard = lax.axis_index(MP), lax.axis_index(DP)
    ring = lax.axis_size("x")
    held = gate_weight.shape[0]
    quota = held // n_mp
    slab = BS // n_dp
    per = tokens.shape[1] // BS
    n_rows = per * n_mp
    owned = column_order.shape[0] // n_mp
    total = 3 * held
    group = total // STEPS
    tok = tokens.shape[0]

    x_all = lax.all_gather(jnp.stack([tokens, grad_out]), MP, axis=0, tiled=False)

    slabs = jnp.stack(
        [
            lax.dynamic_slice_in_dim(w, shard * slab, slab, 1).reshape(n_mp, quota, slab, BS)
            for w in (gate_weight, up_weight, down_weight)
        ],
        axis=1,
    )
    mine = lax.all_to_all(slabs, MP, split_axis=0, concat_axis=0, tiled=True)
    weights = spread(mine.reshape(total, slab, BS))

    tables = jnp.stack([gate_block_pairs, up_blocks, down_blocks])
    tables = tables.reshape(3, n_mp, n_mp, quota, 2)
    tables = lax.dynamic_index_in_dim(tables, member, 2, keepdims=False).transpose(1, 0, 2, 3)
    is_down = (jnp.arange(3) == 2)[None, :, None]
    rows = jnp.where(is_down, tables[..., 1], tables[..., 0]).reshape(total)
    names = jnp.where(is_down, tables[..., 0], tables[..., 1]).reshape(total)
    own_cols = lax.dynamic_slice_in_dim(column_order, member * owned, owned, 0)
    cols = jnp.sum(
        jnp.where(names[:, None] == own_cols[None, :], jnp.arange(owned, dtype=jnp.int32), 0),
        axis=1,
    )
    slots = slots_of().astype(jnp.int32)

    x_spec = full(x_all.shape)
    w_spec = pl.BlockSpec((n_dp, group, slab, BS), lambda g, *_: (0, g, 0, 0))
    act_shape = (3, owned, tok, BS)
    piece = lambda place: pl.BlockSpec((group, slab, BS), lambda g, *_: (place(g), 0, 0))
    early, late = (lambda g: jnp.minimum(g, STEPS // 2 - 1)), (lambda g: jnp.maximum(g - STEPS // 2, 0))
    w_specs = [piece(lambda g: g)] * 2 + [piece(early), piece(late)] * 6
    whole = pltpu.VMEM((group, n_dp, slab, BS), BF)
    params = pltpu.CompilerParams(dimension_semantics=("arbitrary",))

    x_t = pl.pallas_call(
        functools.partial(flip_kernel, per=per),
        out_shape=jax.ShapeDtypeStruct((n_rows, BS, tok), BF),
        grid=(ring,),
        in_specs=[pl.BlockSpec((ring, 1, tok, per * BS), lambda g: (g, 0, 0, 0))],
        out_specs=pl.BlockSpec((ring * per, BS, tok), lambda g: (g, 0, 0)),
        compiler_params=params,
        name="flip",
    )(x_all)

    act, hidden_own = pl.pallas_call(
        functools.partial(sums_kernel, per=per, quota=quota, owned=owned),
        out_shape=(
            jax.ShapeDtypeStruct(act_shape, BF),
            jax.ShapeDtypeStruct((tok, owned * BS), BF),
        ),
        grid_spec=pltpu.PrefetchScalarGridSpec(
            num_scalar_prefetch=3,
            grid=(STEPS,),
            in_specs=[x_spec] + w_specs,
            out_specs=[full(act_shape), full((tok, owned * BS))],
            scratch_shapes=[pltpu.VMEM(act_shape, F32), whole],
        ),
        compiler_params=params,
        name="sums",
    )(rows, cols, slots, x_all, *weights)

    grads = pl.pallas_call(
        functools.partial(grads_kernel, per=per, quota=quota),
        out_shape=jax.ShapeDtypeStruct((n_dp, total, slab, BS), BF),
        grid_spec=pltpu.PrefetchScalarGridSpec(
            num_scalar_prefetch=2,
            grid=(STEPS,),
            in_specs=[full(x_t.shape), x_spec, full(act_shape)],
            out_specs=w_spec,
            scratch_shapes=[pltpu.VMEM((owned, BS, tok), BF)],
        ),
        compiler_params=params,
        name="grads",
    )(rows, cols, x_t, x_all, act)
    grads = lax.psum_scatter(grads, DP, scatter_dimension=0, tiled=True)

    place = jnp.stack([lax.axis_index("x"), lax.axis_index("z")]).astype(jnp.int32)
    part_shape = (ring, tok, per * BS)
    parts = pl.pallas_call(
        functools.partial(parts_kernel, per=per, quota=quota, count=len(weights)),
        out_shape=[jax.ShapeDtypeStruct(part_shape, BF)] * (2 * ring),
        grid_spec=pltpu.PrefetchScalarGridSpec(
            num_scalar_prefetch=4,
            grid=(STEPS,),
            in_specs=[full(act_shape)] + w_specs,
            out_specs=[full(part_shape)] * (2 * ring),
            scratch_shapes=[pltpu.VMEM((2, n_rows, tok, BS), F32), whole],
        ),
        compiler_params=params,
        name="parts",
    )(rows, cols, slots, place, act, *weights)
    output, input_grad = collect(parts[:ring], parts[ring:])

    grads = grads.reshape(n_mp, 3, quota, slab, BS)
    grads = lax.all_to_all(grads, MP, split_axis=0, concat_axis=0, tiled=True)
    gate_grad, up_grad, down_grad = (
        grads[:, p].reshape(held, slab, BS) for p in range(3)
    )
    return (hidden_own, output, input_grad, gate_grad, up_grad, down_grad)


def solution(mesh):
    mesh = Mesh(mesh.devices.reshape(4, 2, 4, 4), DP + MP)
    wide_spec, block_spec, grad_spec = P(DP, MP), P(MP, None, None), P(MP, DP, None)
    return jax.shard_map(
        body,
        mesh=mesh,
        in_specs=(wide_spec,) * 2 + (block_spec,) * 3 + (P(),) * 4,
        out_specs=(wide_spec,) * 3 + (grad_spec,) * 3,
        check_vma=False,
    )
```

```python
import functools

import jax
import jax.numpy as jnp
from jax import lax
from jax.experimental import pallas as pl
from jax.experimental.pallas import tpu as pltpu
from jax.sharding import Mesh, PartitionSpec as P

BS = 128
MP = ("x", "z")
DP = ("y", "c")
BF = jnp.bfloat16
F32 = jnp.float32
SMEM = pl.BlockSpec(memory_space=pltpu.SMEM)
ANY = pl.BlockSpec(memory_space=pl.ANY)
VMEM = pl.BlockSpec(memory_space=pltpu.VMEM)


def dot(a, b):
    return lax.dot_general(a, b, (((1,), (0,)), ((), ())), preferred_element_type=F32)


def dot_t(a, b):
    return lax.dot_general(a, b, (((1,), (1,)), ((), ())), preferred_element_type=F32)


def start_all(pairs, sems, first):
    copies = [pltpu.make_async_copy(a, b, sems.at[first + i]) for i, (a, b) in enumerate(pairs)]
    for copy in copies:
        copy.start()
    return copies


def wait_all(copies):
    for copy in copies:
        copy.wait()


def piece_pairs(slots, pieces, whole):
    half = whole.shape[0] // 2
    own = [(pieces[i], whole.at[:, slots[i]]) for i in range(2)]
    early = [(pieces[2 * i - 2], whole.at[:half, slots[i]]) for i in range(2, 8)]
    late = [(pieces[2 * i - 1], whole.at[half:, slots[i]]) for i in range(2, 8)]
    return own, early, late


def wide(ref, block, per):
    ring = ref.shape[0]
    lane = pl.multiple_of((block % per) * BS, BS)
    near = block // per
    return ref[near // ring, near % ring, :, pl.ds(lane, BS)]


def each_block(low, high, rows, cols, quota, visit):
    def share(i, carry):
        for b in range(3 * quota):
            k = i * 3 * quota + b
            visit(k, b // quota, rows[k], cols[k])
        return carry

    lax.fori_loop(low, high, share, 0)


def owner_kernel(rows, cols, slots, spots, *refs, ring, per, quota, owned, count):
    tokens, grads, pieces = refs[:ring], refs[ring : 2 * ring], refs[2 * ring : 2 * ring + count]
    refs = refs[2 * ring + count :]
    act_ref, own_ref = refs[:2]
    results = refs[2:6]
    tok, cot, flipped, whole, acc, flipped_hidden = refs[6:12]
    stages, sems = refs[12:16], refs[16]
    shares = whole.shape[0] // (3 * quota)
    half = whole.shape[0] // 2

    own, early, late = piece_pairs(slots, pieces, whole)
    tok_copies = start_all([(tokens[t], tok.at[:, t]) for t in range(ring)], sems, 0)
    early_copies = start_all(own + early + [(grads[s], cot.at[s]) for s in range(ring)], sems, ring)
    late_copies = start_all(late, sems, ring + len(early_copies))
    acc[...] = jnp.zeros_like(acc)

    index = lambda d: lax.broadcasted_iota(jnp.int32, (BS, BS), d)
    unit = jnp.where(index(0) == index(1), 1.0, 0.0).astype(BF)
    wait_all(tok_copies)

    def flip(m, carry):
        for q in range(per):
            x = tok[m // ring, m % ring, :, q * BS : (q + 1) * BS]
            flipped[m * per + q] = dot_t(unit, x).astype(BF)
        return carry

    lax.fori_loop(0, ring * ring, flip, 0, unroll=2)

    def add(k, proj, r, c):
        w = whole[k].reshape(BS, BS)
        if proj < 2:
            acc[proj, c] += dot(wide(tok, r, per), w)
        else:
            acc[proj, c] += dot_t(wide(cot, r, per), w)

    wait_all(early_copies)
    each_block(0, shares // 2, rows, cols, quota, add)
    wait_all(late_copies)
    each_block(shares // 2, shares, rows, cols, quota, add)

    for c in range(owned):
        gate, up, grad = acc[0, c], acc[1, c], acc[2, c]
        s = jax.nn.sigmoid(gate)
        silu = gate * s
        hidden = (silu * up).astype(BF)
        act_ref[0, c] = hidden
        own_ref[:, c * BS : (c + 1) * BS] = hidden
        act_ref[1, c] = (grad * up * s * (1.0 + gate * (1.0 - s))).astype(BF)
        act_ref[2, c] = (grad * silu).astype(BF)
        flipped_hidden[c] = dot_t(unit, hidden).astype(BF)

    first_core = slots[0] % 2 == 0
    copies = []
    for part in range(2):
        kept, given = stages[part], stages[2 + part]

        def outer(k, proj, r, c):
            if proj < 2:
                g = dot(flipped[r], act_ref[1 + proj, c])
            else:
                g = dot(flipped_hidden[c], wide(cot, r, per))
            g = g.astype(BF).reshape(ring, 2, BS // (2 * ring), BS)
            keep = jnp.where(first_core, g[:, 0], g[:, 1])
            give = jnp.where(first_core, g[:, 1], g[:, 0])
            for y in range(ring):
                kept[spots[y], k - part * half] = keep[y]
                given[spots[y], k - part * half] = give[y]

        each_block(part * shares // 2, (part + 1) * shares // 2, rows, cols, quota, outer)
        copies += start_all(
            [(given, results[2 + part]), (kept, results[part])],
            sems,
            ring + len(early_copies) + len(late_copies) + 2 * part,
        )
    wait_all(copies)


def parts_kernel(rows, cols, slots, act_ref, *refs, ring, per, quota, count):
    pieces, outs = refs[:count], refs[count : count + 2 * ring]
    acc, whole, stage, sems = refs[count + 2 * ring :]
    shares = whole.shape[0] // (3 * quota)
    own, early, late = piece_pairs(slots, pieces, whole)
    early_copies = start_all(own + early, sems, 0)
    late_copies = start_all(late, sems, len(early_copies))
    acc[...] = jnp.zeros_like(acc)

    def add(k, proj, r, c):
        w = whole[k].reshape(BS, BS)
        if proj < 2:
            acc[1, r] += dot_t(act_ref[1 + proj, c], w)
        else:
            acc[0, r] += dot(act_ref[0, c], w)

    wait_all(early_copies)
    each_block(0, shares // 2, rows, cols, quota, add)
    wait_all(late_copies)
    each_block(shares // 2, shares, rows, cols, quota, add)

    copies = []
    for hop in list(range(1, ring)) + [0]:
        for which in range(2):
            for turn in range(ring):
                near = (hop * ring + turn, turn * ring + hop)[which]
                for q in range(per):
                    stage[which * ring + hop, turn, :, q * BS : (q + 1) * BS] = acc[
                        which, near * per + q
                    ].astype(BF)
            at = which * ring + hop
            copies += start_all(
                [(stage.at[at], outs[at])], sems, len(early_copies) + len(late_copies) + at
            )
    wait_all(copies)


def shift(value, axis, hop):
    size = lax.axis_size(axis)
    return lax.ppermute(value, axis, [(i, (i + hop) % size) for i in range(size)])


def total(*terms):
    return sum(t.astype(F32) for t in terms)


def gather_ring(value, axes):
    ring = lax.axis_size(axes[0])
    line = jnp.stack([value] + [shift(value, axes[0], hop) for hop in range(1, ring)])
    return lambda: [line] + [shift(line, axes[1], hop) for hop in range(1, ring)]


def spread(mine):
    half = mine.shape[0] // 2
    parts = mine[:half], mine[half:]
    up, down = [None] * 2, [None] * 2
    up[0], down[1] = shift(parts[0], "y", 1), shift(parts[1], "y", -1)
    up[1], down[0] = shift(parts[1], "y", 1), shift(parts[0], "y", -1)
    far = [shift(up[0], "y", 1), shift(down[1], "y", -1)]
    swap = lambda value: shift(value, "c", 1)
    pieces = [mine, swap(mine)]
    for pair in (up, down, far):
        pieces += pair + [swap(v) for v in pair]
    return pieces


def fold(keeps, gives):
    ring = lax.axis_size("y")
    done = []
    for keep, give, way in zip(keeps, gives, (1, -1)):
        got = shift(give, "c", 1)
        pair = lambda hop: total(keep[hop % ring], got[hop % ring])
        far = shift(pair(2).astype(BF), "y", way)
        back = shift(pair(-way).astype(BF), "y", -way)
        last = shift(total(pair(way), far).astype(BF), "y", way)
        done.append(total(pair(0), back, last).astype(BF))
    return jnp.concatenate(done)


def collect(outs, grads):
    ring = len(outs)
    first = [[p[0]] + [shift(p[h], a, -h) for h in range(1, ring)] for p, a in ((outs, "x"), (grads, "z"))]
    done = []
    for terms, axis in zip(first, ("z", "x")):
        sums = [total(*[t[turn] for t in terms]) for turn in range(ring)]
        arrived = [shift(sums[turn].astype(BF), axis, -turn) for turn in range(1, ring)]
        done.append(total(sums[0], *arrived).astype(BF))
    return done


def body(
    tokens,
    grad_out,
    gate_weight,
    up_weight,
    down_weight,
    gate_block_pairs,
    up_blocks,
    down_blocks,
    column_order,
):
    n_mp, n_dp = lax.axis_size(MP), lax.axis_size(DP)
    member, shard = lax.axis_index(MP), lax.axis_index(DP)
    x, y, z, core = (lax.axis_index(a) for a in ("x", "y", "z", "c"))
    ring = lax.axis_size("x")
    held = gate_weight.shape[0]
    quota = held // n_mp
    slab = BS // n_dp
    per = tokens.shape[1] // BS
    n_rows = per * n_mp
    owned = column_order.shape[0] // n_mp
    count = 3 * held
    tok = tokens.shape[0]

    send_tokens = gather_ring(tokens, ("x", "z"))
    send_grads = gather_ring(grad_out, ("z", "x"))

    slabs = jnp.stack(
        [
            lax.dynamic_slice_in_dim(w, shard * slab, slab, 1).reshape(n_mp, quota, slab, BS)
            for w in (gate_weight, up_weight, down_weight)
        ],
        axis=1,
    )
    mine = lax.all_to_all(slabs, MP, split_axis=0, concat_axis=0, tiled=True)
    weights = spread(mine.reshape(count, slab, BS))
    token_parts, grad_parts = send_tokens(), send_grads()

    tables = jnp.stack([gate_block_pairs, up_blocks, down_blocks])
    tables = tables.reshape(3, n_mp, n_mp, quota, 2)
    tables = lax.dynamic_index_in_dim(tables, member, 2, keepdims=False).transpose(1, 0, 2, 3)
    is_down = (jnp.arange(3) == 2)[None, :, None]
    rows = jnp.where(is_down, tables[..., 1], tables[..., 0]).reshape(count)
    names = jnp.where(is_down, tables[..., 0], tables[..., 1]).reshape(count)
    near, far = (x + ring - rows // (per * ring)) % ring, (z + ring - rows // per % ring) % ring
    rows = (near * ring + far) * per + rows % per
    own_cols = lax.dynamic_slice_in_dim(column_order, member * owned, owned, 0)
    cols = jnp.sum(
        jnp.where(names[:, None] == own_cols[None, :], jnp.arange(owned, dtype=jnp.int32), 0),
        axis=1,
    )
    slots = jnp.stack(
        [(y + hop + ring) % ring * 2 + c for hop in (0, -1, 1, 2) for c in (core, 1 - core)]
    ).astype(jnp.int32)
    spots = ((jnp.arange(ring) - y + ring) % ring).astype(jnp.int32)

    act_shape = (3, owned, tok, BS)
    x_shape = (ring, ring, tok, per * BS)
    half_shape = (ring, count // 2, slab, BS)
    whole = pltpu.VMEM((count, n_dp, slab, BS), BF)
    sizes = dict(ring=ring, per=per, quota=quota, count=len(weights))

    act, hidden_own, keep_a, keep_b, give_a, give_b = pl.pallas_call(
        functools.partial(owner_kernel, owned=owned, **sizes),
        out_shape=[jax.ShapeDtypeStruct(act_shape, BF), jax.ShapeDtypeStruct((tok, owned * BS), BF)]
        + [jax.ShapeDtypeStruct(half_shape, BF)] * 4,
        in_specs=[SMEM] * 4 + [ANY] * (2 * ring + len(weights)),
        out_specs=[VMEM] * 2 + [ANY] * 4,
        scratch_shapes=[
            pltpu.VMEM(x_shape, BF),
            pltpu.VMEM(x_shape, BF),
            pltpu.VMEM((n_rows, BS, tok), BF),
            whole,
            pltpu.VMEM(act_shape, F32),
            pltpu.VMEM((owned, BS, tok), BF),
        ]
        + [pltpu.VMEM(half_shape, BF)] * 4
        + [pltpu.SemaphoreType.DMA((2 * ring + len(weights) + 4,))],
        name="owner",
    )(rows, cols, slots, spots, *token_parts, *grad_parts, *weights)

    part_shape = (ring, tok, per * BS)
    parts = pl.pallas_call(
        functools.partial(parts_kernel, **sizes),
        out_shape=[jax.ShapeDtypeStruct(part_shape, BF)] * (2 * ring),
        in_specs=[SMEM] * 3 + [VMEM] + [ANY] * len(weights),
        out_specs=[ANY] * (2 * ring),
        scratch_shapes=[
            pltpu.VMEM((2, n_rows, tok, BS), F32),
            whole,
            pltpu.VMEM((2 * ring,) + part_shape, BF),
            pltpu.SemaphoreType.DMA((len(weights) + 2 * ring,)),
        ],
        name="parts",
    )(rows, cols, slots, act, *weights)

    grads = fold((keep_a, keep_b), (give_a, give_b))
    output, input_grad = collect(parts[:ring], parts[ring:])
    grads = grads.reshape(n_mp, 3, quota, slab, BS)
    grads = lax.all_to_all(grads, MP, split_axis=0, concat_axis=0, tiled=True)
    gate_grad, up_grad, down_grad = (grads[:, p].reshape(held, slab, BS) for p in range(3))
    return (hidden_own, output, input_grad, gate_grad, up_grad, down_grad)


def solution(mesh):
    mesh = Mesh(mesh.devices.reshape(4, 2, 4, 4), DP + MP)
    wide_spec, block_spec, grad_spec = P(DP, MP), P(MP, None, None), P(MP, DP, None)
    return jax.shard_map(
        body,
        mesh=mesh,
        in_specs=(wide_spec,) * 2 + (block_spec,) * 3 + (P(),) * 4,
        out_specs=(wide_spec,) * 3 + (grad_spec,) * 3,
        check_vma=False,
    )
```

```python
import functools

import jax
import jax.numpy as jnp
from jax import lax
from jax.experimental import pallas as pl
from jax.experimental.pallas import tpu as pltpu
from jax.sharding import Mesh, PartitionSpec as P

BS = 128
MP = ("x", "z")
DP = ("y", "c")
BF = jnp.bfloat16
F32 = jnp.float32
SMEM = pl.BlockSpec(memory_space=pltpu.SMEM)
ANY = pl.BlockSpec(memory_space=pl.ANY)
VMEM = pl.BlockSpec(memory_space=pltpu.VMEM)


def dot(a, b):
    return lax.dot_general(a, b, (((1,), (0,)), ((), ())), preferred_element_type=F32)


def dot_t(a, b):
    return lax.dot_general(a, b, (((1,), (1,)), ((), ())), preferred_element_type=F32)


def start_all(pairs, sems, first):
    copies = [pltpu.make_async_copy(a, b, sems.at[first + i]) for i, (a, b) in enumerate(pairs)]
    for copy in copies:
        copy.start()
    return copies


def wait_all(copies):
    for copy in copies:
        copy.wait()


def piece_pairs(slots, pieces, whole):
    half = whole.shape[0] // 2
    own = [(pieces[i], whole.at[:, slots[i]]) for i in range(2)]
    early = [(pieces[2 * i - 2], whole.at[:half, slots[i]]) for i in range(2, 8)]
    late = [(pieces[2 * i - 1], whole.at[half:, slots[i]]) for i in range(2, 8)]
    return own, early, late


def wide(ref, block, per):
    lane = pl.multiple_of((block % per) * BS, BS)
    return ref[block // per, :, pl.ds(lane, BS)]


def each_block(low, high, rows, cols, quota, visit):
    def share(i, carry):
        for b in range(3 * quota):
            k = i * 3 * quota + b
            visit(k, b // quota, rows[k], cols[k])
        return carry

    lax.fori_loop(low, high, share, 0)


def owner_kernel(rows, cols, slots, x_all, *refs, per, quota, owned, count):
    pieces, refs = refs[:count], refs[count:]
    act_ref, own_ref, result = refs[:3]
    tok, cot, flipped, whole, acc, flipped_hidden, stage, sems = refs[3:]
    shares, members = whole.shape[0] // (3 * quota), tok.shape[0]
    half, line = whole.shape[0] // 2, members // 4

    def quarters(which, ref):
        return [(x_all.at[i * line : (i + 1) * line, which], ref.at[i * line : (i + 1) * line]) for i in range(4)]

    own, early, late = piece_pairs(slots, pieces, whole)
    tok_copies = start_all(quarters(0, tok), sems, 0)
    early_copies = start_all(own + early + quarters(1, cot), sems, 4)
    late_copies = start_all(late, sems, 4 + len(early_copies))
    acc[...] = jnp.zeros_like(acc)

    index = lambda d: lax.broadcasted_iota(jnp.int32, (BS, BS), d)
    unit = jnp.where(index(0) == index(1), 1.0, 0.0).astype(BF)

    def flip(m, carry):
        for q in range(per):
            x = tok[m, :, q * BS : (q + 1) * BS]
            flipped[m * per + q] = dot_t(unit, x).astype(BF)
        return carry

    for i, copy in enumerate(tok_copies):
        copy.wait()
        lax.fori_loop(i * line, (i + 1) * line, flip, 0, unroll=2)

    def add(k, proj, r, c):
        w = whole[k].reshape(BS, BS)
        if proj < 2:
            acc[proj, c] += dot(wide(tok, r, per), w)
        else:
            acc[proj, c] += dot_t(wide(cot, r, per), w)

    wait_all(early_copies)
    each_block(0, shares // 2, rows, cols, quota, add)
    wait_all(late_copies)
    each_block(shares // 2, shares, rows, cols, quota, add)

    for c in range(owned):
        gate, up, grad = acc[0, c], acc[1, c], acc[2, c]
        s = jax.nn.sigmoid(gate)
        silu = gate * s
        hidden = (silu * up).astype(BF)
        act_ref[0, c] = hidden
        own_ref[:, c * BS : (c + 1) * BS] = hidden
        act_ref[1, c] = (grad * up * s * (1.0 + gate * (1.0 - s))).astype(BF)
        act_ref[2, c] = (grad * silu).astype(BF)
        flipped_hidden[c] = dot_t(unit, hidden).astype(BF)

    def outer(k, proj, r, c):
        if proj < 2:
            g = dot(flipped[r], act_ref[1 + proj, c])
        else:
            g = dot(flipped_hidden[c], wide(cot, r, per))
        stage[:, k] = g.astype(BF).reshape(stage.shape[0], -1, BS)

    copies = []
    for part in range(4):
        each_block(part * shares // 4, (part + 1) * shares // 4, rows, cols, quota, outer)
        at = pl.ds(part * half // 2, half // 2)
        copies += start_all(
            [(stage.at[:, at], result.at[:, at])],
            sems,
            4 + len(early_copies) + len(late_copies) + part,
        )
    wait_all(copies)


def parts_kernel(rows, cols, slots, act_ref, *refs, ring, per, quota, count):
    pieces, outs = refs[:count], refs[count : count + 2 * ring]
    acc, whole, stage, sems = refs[count + 2 * ring :]
    shares = whole.shape[0] // (3 * quota)
    own, early, late = piece_pairs(slots, pieces, whole)
    early_copies = start_all(own + early, sems, 0)
    late_copies = start_all(late, sems, len(early_copies))
    acc[...] = jnp.zeros_like(acc)

    def add(k, proj, r, c):
        w = whole[k].reshape(BS, BS)
        if proj < 2:
            acc[1, r] += dot_t(act_ref[1 + proj, c], w)
        else:
            acc[0, r] += dot(act_ref[0, c], w)

    wait_all(early_copies)
    each_block(0, shares // 2, rows, cols, quota, add)
    wait_all(late_copies)
    each_block(shares // 2, shares, rows, cols, quota, add)

    copies = []
    for hop in list(range(1, ring)) + [0]:
        for which in range(2):
            for turn in range(ring):
                near = (hop * ring + turn, turn * ring + hop)[which]
                for q in range(per):
                    stage[which * ring + hop, turn, :, q * BS : (q + 1) * BS] = acc[
                        which, near * per + q
                    ].astype(BF)
            at = which * ring + hop
            copies += start_all(
                [(stage.at[at], outs[at])], sems, len(early_copies) + len(late_copies) + at
            )
    wait_all(copies)


def shift(value, axis, hop):
    size = lax.axis_size(axis)
    return lax.ppermute(value, axis, [(i, (i + hop) % size) for i in range(size)])


def total(*terms):
    return sum(t.astype(F32) for t in terms)


def spread(mine):
    half = mine.shape[0] // 2
    parts = mine[:half], mine[half:]
    up, down = [None] * 2, [None] * 2
    up[0], down[1] = shift(parts[0], "y", 1), shift(parts[1], "y", -1)
    up[1], down[0] = shift(parts[1], "y", 1), shift(parts[0], "y", -1)
    far = [shift(up[0], "y", 1), shift(down[1], "y", -1)]
    swap = lambda value: shift(value, "c", 1)
    pieces = [mine, swap(mine)]
    for pair in (up, down, far):
        pieces += pair + [swap(v) for v in pair]
    return pieces


def collect(outs, grads):
    ring = len(outs)
    first = [[p[0]] + [shift(p[h], a, -h) for h in range(1, ring)] for p, a in ((outs, "x"), (grads, "z"))]
    done = []
    for terms, axis in zip(first, ("z", "x")):
        sums = [total(*[t[turn] for t in terms]) for turn in range(ring)]
        arrived = [shift(sums[turn].astype(BF), axis, -turn) for turn in range(1, ring)]
        done.append(total(sums[0], *arrived).astype(BF))
    return done


def body(
    tokens,
    grad_out,
    gate_weight,
    up_weight,
    down_weight,
    gate_block_pairs,
    up_blocks,
    down_blocks,
    column_order,
):
    n_mp, n_dp = lax.axis_size(MP), lax.axis_size(DP)
    member, shard = lax.axis_index(MP), lax.axis_index(DP)
    x, y, z, core = (lax.axis_index(a) for a in ("x", "y", "z", "c"))
    ring = lax.axis_size("x")
    held = gate_weight.shape[0]
    quota = held // n_mp
    slab = BS // n_dp
    per = tokens.shape[1] // BS
    n_rows = per * n_mp
    owned = column_order.shape[0] // n_mp
    count = 3 * held
    tok = tokens.shape[0]

    x_all = lax.all_gather(jnp.stack([tokens, grad_out]), MP, axis=0, tiled=False)

    slabs = jnp.stack(
        [
            lax.dynamic_slice_in_dim(w, shard * slab, slab, 1).reshape(n_mp, quota, slab, BS)
            for w in (gate_weight, up_weight, down_weight)
        ],
        axis=1,
    )
    mine = lax.all_to_all(slabs, MP, split_axis=0, concat_axis=0, tiled=True)
    weights = spread(mine.reshape(count, slab, BS))

    tables = jnp.stack([gate_block_pairs, up_blocks, down_blocks])
    tables = tables.reshape(3, n_mp, n_mp, quota, 2)
    tables = lax.dynamic_index_in_dim(tables, member, 2, keepdims=False).transpose(1, 0, 2, 3)
    is_down = (jnp.arange(3) == 2)[None, :, None]
    rows = jnp.where(is_down, tables[..., 1], tables[..., 0]).reshape(count)
    names = jnp.where(is_down, tables[..., 0], tables[..., 1]).reshape(count)
    near, far = (x + ring - rows // (per * ring)) % ring, (z + ring - rows // per % ring) % ring
    hops = (near * ring + far) * per + rows % per
    own_cols = lax.dynamic_slice_in_dim(column_order, member * owned, owned, 0)
    cols = jnp.sum(
        jnp.where(names[:, None] == own_cols[None, :], jnp.arange(owned, dtype=jnp.int32), 0),
        axis=1,
    )
    slots = jnp.stack(
        [(y + hop + ring) % ring * 2 + c for hop in (0, -1, 1, 2) for c in (core, 1 - core)]
    ).astype(jnp.int32)

    act_shape = (3, owned, tok, BS)
    x_shape = (n_mp, tok, per * BS)
    grad_shape = (n_dp, count, slab, BS)
    whole = pltpu.VMEM((count, n_dp, slab, BS), BF)
    sizes = dict(per=per, quota=quota, count=len(weights))

    act, hidden_own, grads = pl.pallas_call(
        functools.partial(owner_kernel, owned=owned, **sizes),
        out_shape=[jax.ShapeDtypeStruct(act_shape, BF), jax.ShapeDtypeStruct((tok, owned * BS), BF)]
        + [jax.ShapeDtypeStruct(grad_shape, BF)],
        in_specs=[SMEM] * 3 + [ANY] * (1 + len(weights)),
        out_specs=[VMEM] * 2 + [ANY],
        scratch_shapes=[
            pltpu.VMEM(x_shape, BF),
            pltpu.VMEM(x_shape, BF),
            pltpu.VMEM((n_rows, BS, tok), BF),
            whole,
            pltpu.VMEM(act_shape, F32),
            pltpu.VMEM((owned, BS, tok), BF),
            pltpu.VMEM(grad_shape, BF),
            pltpu.SemaphoreType.DMA((len(weights) + 12,)),
        ],
        name="owner",
    )(rows, cols, slots, x_all, *weights)
    grads = lax.psum_scatter(grads, DP, scatter_dimension=0, tiled=True)

    part_shape = (ring, tok, per * BS)
    parts = pl.pallas_call(
        functools.partial(parts_kernel, ring=ring, **sizes),
        out_shape=[jax.ShapeDtypeStruct(part_shape, BF)] * (2 * ring),
        in_specs=[SMEM] * 3 + [VMEM] + [ANY] * len(weights),
        out_specs=[ANY] * (2 * ring),
        scratch_shapes=[
            pltpu.VMEM((2, n_rows, tok, BS), F32),
            whole,
            pltpu.VMEM((2 * ring,) + part_shape, BF),
            pltpu.SemaphoreType.DMA((len(weights) + 2 * ring,)),
        ],
        name="parts",
    )(hops, cols, slots, act, *weights)

    output, input_grad = collect(parts[:ring], parts[ring:])
    grads = grads.reshape(n_mp, 3, quota, slab, BS)
    grads = lax.all_to_all(grads, MP, split_axis=0, concat_axis=0, tiled=True)
    gate_grad, up_grad, down_grad = (grads[:, p].reshape(held, slab, BS) for p in range(3))
    return (hidden_own, output, input_grad, gate_grad, up_grad, down_grad)


def solution(mesh):
    mesh = Mesh(mesh.devices.reshape(4, 2, 4, 4), DP + MP)
    wide_spec, block_spec, grad_spec = P(DP, MP), P(MP, None, None), P(MP, DP, None)
    return jax.shard_map(
        body,
        mesh=mesh,
        in_specs=(wide_spec,) * 2 + (block_spec,) * 3 + (P(),) * 4,
        out_specs=(wide_spec,) * 3 + (grad_spec,) * 3,
        check_vma=False,
    )
```

```python
import functools

import jax
import jax.numpy as jnp
from jax import lax
from jax.experimental import pallas as pl
from jax.experimental.pallas import tpu as pltpu
from jax.sharding import Mesh, PartitionSpec as P

BS = 128
UNROLL = 4
MP = ("x", "z")
DP = ("y", "c")
BF = jnp.bfloat16
F32 = jnp.float32
SMEM = pl.BlockSpec(memory_space=pltpu.SMEM)
ANY = pl.BlockSpec(memory_space=pl.ANY)
VMEM = pl.BlockSpec(memory_space=pltpu.VMEM)


def dot(a, b):
    return lax.dot_general(a, b, (((1,), (0,)), ((), ())), preferred_element_type=F32)


def dot_t(a, b):
    return lax.dot_general(a, b, (((1,), (1,)), ((), ())), preferred_element_type=F32)


def start_all(pairs, sems, first):
    copies = [pltpu.make_async_copy(a, b, sems.at[first + i]) for i, (a, b) in enumerate(pairs)]
    for copy in copies:
        copy.start()
    return copies


def wait_all(copies):
    for copy in copies:
        copy.wait()


def piece_pairs(slots, pieces, whole):
    half = whole.shape[0] // 2
    at = lambda part, i: whole.at[(part,) + (slice(None),) * (len(whole.shape) - 4) + (slots[i],)]
    own = [(pieces[i], at(slice(None), i)) for i in range(2)]
    early = [(pieces[2 * i - 2], at(slice(half), i)) for i in range(2, 8)]
    late = [(pieces[2 * i - 1], at(slice(half, 2 * half), i)) for i in range(2, 8)]
    return own, early, late


def wide(ref, block, per):
    lane = pl.multiple_of((block & (per - 1)) * BS, BS)
    return ref[block >> (per.bit_length() - 1), :, pl.ds(lane, BS)]


def each_block(low, high, rows, cols, quota, projections, visit):
    def share(i, carry):
        for proj in projections:
            for b in range(quota):
                k = (i * 3 + proj) * quota + b
                visit((i, proj, b), k, rows[k], cols[k])
        return carry

    lax.fori_loop(low, high, share, 0, unroll=UNROLL)


def owner_kernel(rows, cols, slots, x_all, *refs, per, quota, owned, count):
    pieces, refs = refs[:count], refs[count:]
    act_ref, own_ref, result = refs[:3]
    tok, cot, flipped, whole, acc, flipped_hidden, stage, sems = refs[3:]
    shares, members = whole.shape[0] // (3 * quota), tok.shape[0]
    half, line = whole.shape[0] // 2, members // 4

    def quarters(which, ref):
        return [(x_all.at[i * line : (i + 1) * line, which], ref.at[i * line : (i + 1) * line]) for i in range(4)]

    own, early, late = piece_pairs(slots, pieces, whole)
    tok_copies = start_all(quarters(0, tok), sems, 0)
    early_copies = start_all(own + early + quarters(1, cot), sems, 4)
    late_copies = start_all(late, sems, 4 + len(early_copies))
    acc[...] = jnp.zeros_like(acc)

    index = lambda d: lax.broadcasted_iota(jnp.int32, (BS, BS), d)
    unit = jnp.where(index(0) == index(1), 1.0, 0.0).astype(BF)

    def flip(m, carry):
        for q in range(per):
            x = tok[m, :, q * BS : (q + 1) * BS]
            flipped[m * per + q] = dot_t(unit, x).astype(BF)
        return carry

    for i, copy in enumerate(tok_copies):
        copy.wait()
        lax.fori_loop(i * line, (i + 1) * line, flip, 0, unroll=2)

    def add(at, k, r, c):
        proj, w = at[1], whole[k].reshape(BS, BS)
        if proj < 2:
            acc[proj, c] += dot(wide(tok, r, per), w)
        else:
            acc[proj, c] += dot_t(wide(cot, r, per), w)

    wait_all(early_copies)
    each_block(0, shares // 2, rows, cols, quota, range(3), add)
    wait_all(late_copies)
    each_block(shares // 2, shares, rows, cols, quota, range(3), add)

    for c in range(owned):
        gate, up, grad = acc[0, c], acc[1, c], acc[2, c]
        s = jax.nn.sigmoid(gate)
        silu = gate * s
        hidden = (silu * up).astype(BF)
        act_ref[0, c] = hidden
        own_ref[:, c * BS : (c + 1) * BS] = hidden
        act_ref[1, c] = (grad * up * s * (1.0 + gate * (1.0 - s))).astype(BF)
        act_ref[2, c] = (grad * silu).astype(BF)
        flipped_hidden[c] = dot_t(unit, hidden).astype(BF)

    def outer(at, k, r, c):
        if at[1] < 2:
            g = dot(flipped[r], act_ref[1 + at[1], c])
        else:
            g = dot(flipped_hidden[c], wide(cot, r, per))
        stage[:, k] = g.astype(BF).reshape(stage.shape[0], -1, BS)

    copies = []
    for part in range(4):
        each_block(part * shares // 4, (part + 1) * shares // 4, rows, cols, quota, range(3), outer)
        at = pl.ds(part * half // 2, half // 2)
        copies += start_all(
            [(stage.at[:, at], result.at[:, at])],
            sems,
            4 + len(early_copies) + len(late_copies) + part,
        )
    wait_all(copies)


def parts_kernel(rows, cols, slots, act_ref, *refs, ring, per, quota, count, projections):
    pieces, outs = refs[:count], refs[count : count + ring]
    acc, whole, stage, sems = refs[count + ring :]
    shares = whole.shape[0]
    some = slice(projections[0], projections[-1] + 1)
    own, early, late = [
        [(piece.at[:, some], place) for piece, place in pairs]
        for pairs in piece_pairs(slots, pieces, whole)
    ]
    early_copies = start_all(own + early, sems, 0)
    late_copies = start_all(late, sems, len(early_copies))
    acc[...] = jnp.zeros_like(acc)

    def add(at, k, r, c):
        w = whole[at[0], at[1] - projections[0], at[2]].reshape(BS, BS)
        if at[1] < 2:
            acc[r] += dot_t(act_ref[1 + at[1], c], w)
        else:
            acc[r] += dot(act_ref[0, c], w)

    wait_all(early_copies)
    each_block(0, shares // 2, rows, cols, quota, projections, add)
    wait_all(late_copies)
    each_block(shares // 2, shares, rows, cols, quota, projections, add)

    copies = []
    for hop in list(range(1, ring)) + [0]:
        for turn in range(ring):
            near = turn * ring + hop if projections[0] < 2 else hop * ring + turn
            for q in range(per):
                stage[hop, turn, :, q * BS : (q + 1) * BS] = acc[near * per + q].astype(BF)
        copies += start_all([(stage.at[hop], outs[hop])], sems, count + hop)
    wait_all(copies)


def shift(value, axis, hop):
    size = lax.axis_size(axis)
    return lax.ppermute(value, axis, [(i, (i + hop) % size) for i in range(size)])


def total(*terms):
    return sum(t.astype(F32) for t in terms)


def spread(mine):
    half = mine.shape[0] // 2
    parts = mine[:half], mine[half:]
    up, down = [None] * 2, [None] * 2
    up[0], down[1] = shift(parts[0], "y", 1), shift(parts[1], "y", -1)
    up[1], down[0] = shift(parts[1], "y", 1), shift(parts[0], "y", -1)
    far = [shift(up[0], "y", 1), shift(down[1], "y", -1)]
    swap = lambda value: shift(value, "c", 1)
    pieces = [mine, swap(mine)]
    for pair in (up, down, far):
        pieces += pair + [swap(v) for v in pair]
    return pieces


def collect(outs, grads):
    ring = len(outs)
    first = [[p[0]] + [shift(p[h], a, -h) for h in range(1, ring)] for p, a in ((outs, "x"), (grads, "z"))]
    done = []
    for terms, axis in zip(first, ("z", "x")):
        sums = [total(*[t[turn] for t in terms]) for turn in range(ring)]
        arrived = [shift(sums[turn].astype(BF), axis, -turn) for turn in range(1, ring)]
        done.append(total(sums[0], *arrived).astype(BF))
    return done


def body(
    tokens,
    grad_out,
    gate_weight,
    up_weight,
    down_weight,
    gate_block_pairs,
    up_blocks,
    down_blocks,
    column_order,
):
    n_mp, n_dp = lax.axis_size(MP), lax.axis_size(DP)
    member, shard = lax.axis_index(MP), lax.axis_index(DP)
    x, y, z, core = (lax.axis_index(a) for a in ("x", "y", "z", "c"))
    ring = lax.axis_size("x")
    held = gate_weight.shape[0]
    quota = held // n_mp
    slab = BS // n_dp
    per = tokens.shape[1] // BS
    n_rows = per * n_mp
    owned = column_order.shape[0] // n_mp
    count = 3 * held
    tok = tokens.shape[0]

    x_all = lax.all_gather(jnp.stack([tokens, grad_out]), MP, axis=0, tiled=False)

    slabs = jnp.stack(
        [
            lax.dynamic_slice_in_dim(w, shard * slab, slab, 1).reshape(n_mp, quota, slab, BS)
            for w in (gate_weight, up_weight, down_weight)
        ],
        axis=1,
    )
    mine = lax.all_to_all(slabs, MP, split_axis=0, concat_axis=0, tiled=True)
    weights = spread(mine.reshape(count, slab, BS))

    tables = jnp.stack([gate_block_pairs, up_blocks, down_blocks])
    tables = tables.reshape(3, n_mp, n_mp, quota, 2)
    tables = lax.dynamic_index_in_dim(tables, member, 2, keepdims=False).transpose(1, 0, 2, 3)
    is_down = (jnp.arange(3) == 2)[None, :, None]
    rows = jnp.where(is_down, tables[..., 1], tables[..., 0]).reshape(count)
    names = jnp.where(is_down, tables[..., 0], tables[..., 1]).reshape(count)
    near, far = (x + ring - rows // (per * ring)) % ring, (z + ring - rows // per % ring) % ring
    hops = (near * ring + far) * per + rows % per
    own_cols = lax.dynamic_slice_in_dim(column_order, member * owned, owned, 0)
    cols = jnp.sum(
        jnp.where(names[:, None] == own_cols[None, :], jnp.arange(owned, dtype=jnp.int32), 0),
        axis=1,
    )
    slots = jnp.stack(
        [(y + hop + ring) % ring * 2 + c for hop in (0, -1, 1, 2) for c in (core, 1 - core)]
    ).astype(jnp.int32)

    act_shape = (3, owned, tok, BS)
    x_shape = (n_mp, tok, per * BS)
    grad_shape = (n_dp, count, slab, BS)
    whole = pltpu.VMEM((count, n_dp, slab, BS), BF)
    sizes = dict(per=per, quota=quota, count=len(weights))

    act, hidden_own, grads = pl.pallas_call(
        functools.partial(owner_kernel, owned=owned, **sizes),
        out_shape=[jax.ShapeDtypeStruct(act_shape, BF), jax.ShapeDtypeStruct((tok, owned * BS), BF)]
        + [jax.ShapeDtypeStruct(grad_shape, BF)],
        in_specs=[SMEM] * 3 + [ANY] * (1 + len(weights)),
        out_specs=[VMEM] * 2 + [ANY],
        scratch_shapes=[
            pltpu.VMEM(x_shape, BF),
            pltpu.VMEM(x_shape, BF),
            pltpu.VMEM((n_rows, BS, tok), BF),
            whole,
            pltpu.VMEM(act_shape, F32),
            pltpu.VMEM((owned, BS, tok), BF),
            pltpu.VMEM(grad_shape, BF),
            pltpu.SemaphoreType.DMA((len(weights) + 12,)),
        ],
        name="owner",
    )(rows, cols, slots, x_all, *weights)
    grads = lax.psum_scatter(grads, DP, scatter_dimension=0, tiled=True)

    part_shape = (ring, tok, per * BS)
    by_share = [w.reshape(-1, 3, quota, slab, BS) for w in weights]

    def parts_of(projections, name):
        return pl.pallas_call(
            functools.partial(parts_kernel, ring=ring, projections=projections, **sizes),
            out_shape=[jax.ShapeDtypeStruct(part_shape, BF)] * ring,
            in_specs=[SMEM] * 3 + [VMEM] + [ANY] * len(weights),
            out_specs=[ANY] * ring,
            scratch_shapes=[
                pltpu.VMEM((n_rows, tok, BS), F32),
                pltpu.VMEM((n_mp, len(projections), quota, n_dp, slab, BS), BF),
                pltpu.VMEM((ring,) + part_shape, BF),
                pltpu.SemaphoreType.DMA((len(weights) + ring,)),
            ],
            name=name,
        )(hops, cols, slots, act, *by_share)

    out_parts, in_parts = parts_of((2,), "outparts"), parts_of((0, 1), "inparts")
    output, input_grad = collect(out_parts, in_parts)
    grads = grads.reshape(n_mp, 3, quota, slab, BS)
    grads = lax.all_to_all(grads, MP, split_axis=0, concat_axis=0, tiled=True)
    gate_grad, up_grad, down_grad = (grads[:, p].reshape(held, slab, BS) for p in range(3))
    return (hidden_own, output, input_grad, gate_grad, up_grad, down_grad)


def solution(mesh):
    mesh = Mesh(mesh.devices.reshape(4, 2, 4, 4), DP + MP)
    wide_spec, block_spec, grad_spec = P(DP, MP), P(MP, None, None), P(MP, DP, None)
    return jax.shard_map(
        body,
        mesh=mesh,
        in_specs=(wide_spec,) * 2 + (block_spec,) * 3 + (P(),) * 4,
        out_specs=(wide_spec,) * 3 + (grad_spec,) * 3,
        check_vma=False,
    )
```

```python
import functools

import jax
import jax.numpy as jnp
from jax import lax
from jax.experimental import pallas as pl
from jax.experimental.pallas import tpu as pltpu
from jax.sharding import Mesh, PartitionSpec as P

BS = 128
UNROLL = 4
MP = ("x", "z")
DP = ("y", "c")
BF = jnp.bfloat16
F32 = jnp.float32
SMEM = pl.BlockSpec(memory_space=pltpu.SMEM)
ANY = pl.BlockSpec(memory_space=pl.ANY)
VMEM = pl.BlockSpec(memory_space=pltpu.VMEM)


def dot(a, b):
    return lax.dot_general(a, b, (((1,), (0,)), ((), ())), preferred_element_type=F32)


def dot_t(a, b):
    return lax.dot_general(a, b, (((1,), (1,)), ((), ())), preferred_element_type=F32)


def start_all(pairs, sems, first):
    copies = [pltpu.make_async_copy(a, b, sems.at[first + i]) for i, (a, b) in enumerate(pairs)]
    for copy in copies:
        copy.start()
    return copies


def wait_all(copies):
    for copy in copies:
        copy.wait()


def piece_pairs(slots, pieces, whole):
    half = whole.shape[0] // 2
    at = lambda part, i: whole.at[(part,) + (slice(None),) * (len(whole.shape) - 4) + (slots[i],)]
    own = [(pieces[i], at(slice(None), i)) for i in range(2)]
    early = [(pieces[2 * i - 2], at(slice(half), i)) for i in range(2, 8)]
    late = [(pieces[2 * i - 1], at(slice(half, 2 * half), i)) for i in range(2, 8)]
    return own, early, late


def wide(ref, block, per):
    lane = pl.multiple_of((block & (per - 1)) * BS, BS)
    return ref[block >> (per.bit_length() - 1), :, pl.ds(lane, BS)]


def each_block(low, high, rows, cols, quota, projections, visit):
    def share(i, carry):
        for proj in projections:
            for b in range(quota):
                k = (i * 3 + proj) * quota + b
                visit((i, proj, b), k, rows[k], cols[k])
        return carry

    lax.fori_loop(low, high, share, 0, unroll=UNROLL)


def owner_kernel(rows, cols, slots, x_all, *refs, per, quota, owned, count):
    pieces, refs = refs[:count], refs[count:]
    act_ref, own_ref, result = refs[:3]
    tok, cot, flipped, whole, acc, flipped_hidden, stage, sems = refs[3:]
    shares, members = whole.shape[0] // (3 * quota), tok.shape[0]
    half, line = whole.shape[0] // 2, members // 4

    def quarters(which, ref):
        return [(x_all.at[i * line : (i + 1) * line, which], ref.at[i * line : (i + 1) * line]) for i in range(4)]

    own, early, late = piece_pairs(slots, pieces, whole)
    tok_copies = start_all(quarters(0, tok), sems, 0)
    early_copies = start_all(own + early + quarters(1, cot), sems, 4)
    late_copies = start_all(late, sems, 4 + len(early_copies))
    acc[...] = jnp.zeros_like(acc)

    index = lambda d: lax.broadcasted_iota(jnp.int32, (BS, BS), d)
    unit = jnp.where(index(0) == index(1), 1.0, 0.0).astype(BF)

    def flip(m, carry):
        for q in range(per):
            x = tok[m, :, q * BS : (q + 1) * BS]
            flipped[m * per + q] = dot_t(unit, x).astype(BF)
        return carry

    for i, copy in enumerate(tok_copies):
        copy.wait()
        lax.fori_loop(i * line, (i + 1) * line, flip, 0, unroll=2)

    def add(at, k, r, c):
        proj, w = at[1], whole[k].reshape(BS, BS)
        if proj < 2:
            acc[proj, c] += dot(wide(tok, r, per), w)
        else:
            acc[proj, c] += dot_t(wide(cot, r, per), w)

    wait_all(early_copies)
    each_block(0, shares // 2, rows, cols, quota, range(3), add)
    wait_all(late_copies)
    each_block(shares // 2, shares, rows, cols, quota, range(3), add)

    for c in range(owned):
        gate, up, grad = acc[0, c], acc[1, c], acc[2, c]
        s = jax.nn.sigmoid(gate)
        silu = gate * s
        hidden = (silu * up).astype(BF)
        act_ref[0, c] = hidden
        own_ref[:, c * BS : (c + 1) * BS] = hidden
        act_ref[1, c] = (grad * up * s * (1.0 + gate * (1.0 - s))).astype(BF)
        act_ref[2, c] = (grad * silu).astype(BF)
        flipped_hidden[c] = dot_t(unit, hidden).astype(BF)

    def outer(at, k, r, c):
        if at[1] < 2:
            g = dot(flipped[r], act_ref[1 + at[1], c])
        else:
            g = dot(flipped_hidden[c], wide(cot, r, per))
        stage[:, k] = g.astype(BF).reshape(stage.shape[0], -1, BS)

    copies = []
    for part in range(4):
        each_block(part * shares // 4, (part + 1) * shares // 4, rows, cols, quota, range(3), outer)
        at = pl.ds(part * half // 2, half // 2)
        copies += start_all(
            [(stage.at[:, at], result.at[:, at])],
            sems,
            4 + len(early_copies) + len(late_copies) + part,
        )
    wait_all(copies)


def parts_kernel(rows, cols, slots, act_ref, *refs, ring, per, quota, count, projections):
    pieces, outs = refs[:count], refs[count : count + ring]
    acc, whole, stage, sems = refs[count + ring :]
    shares = whole.shape[0]
    some = slice(projections[0], projections[-1] + 1)
    own, early, late = [
        [(piece.at[:, some], place) for piece, place in pairs]
        for pairs in piece_pairs(slots, pieces, whole)
    ]
    early_copies = start_all(own + early, sems, 0)
    late_copies = start_all(late, sems, len(early_copies))
    acc[...] = jnp.zeros_like(acc)

    def add(at, k, r, c):
        w = whole[at[0], at[1] - projections[0], at[2]].reshape(BS, BS)
        if at[1] < 2:
            acc[r] += dot_t(act_ref[1 + at[1], c], w)
        else:
            acc[r] += dot(act_ref[0, c], w)

    wait_all(early_copies)
    each_block(0, shares // 2, rows, cols, quota, projections, add)
    wait_all(late_copies)
    each_block(shares // 2, shares, rows, cols, quota, projections, add)

    copies = []
    for hop in list(range(1, ring)) + [0]:
        for turn in range(ring):
            near = turn * ring + hop if projections[0] < 2 else hop * ring + turn
            for q in range(per):
                stage[hop, turn, :, q * BS : (q + 1) * BS] = acc[near * per + q].astype(BF)
        copies += start_all([(stage.at[hop], outs[hop])], sems, count + hop)
    wait_all(copies)


def shift(value, axis, hop):
    size = lax.axis_size(axis)
    return lax.ppermute(value, axis, [(i, (i + hop) % size) for i in range(size)])


def total(*terms):
    return sum(t.astype(F32) for t in terms)


def spread(mine):
    half = mine.shape[0] // 2
    parts = mine[:half], mine[half:]
    up, down = [None] * 2, [None] * 2
    up[0], down[1] = shift(parts[0], "y", 1), shift(parts[1], "y", -1)
    up[1], down[0] = shift(parts[1], "y", 1), shift(parts[0], "y", -1)
    far = [shift(up[0], "y", 1), shift(down[1], "y", -1)]
    swap = lambda value: shift(value, "c", 1)
    pieces = [mine, swap(mine)]
    for pair in (up, down, far):
        pieces += pair + [swap(v) for v in pair]
    return pieces


def collect(outs, grads):
    ring = len(outs)
    first = [[p[0]] + [shift(p[h], a, -h) for h in range(1, ring)] for p, a in ((outs, "x"), (grads, "z"))]
    done = []
    for terms, axis in zip(first, ("z", "x")):
        sums = [total(*[t[turn] for t in terms]) for turn in range(ring)]
        arrived = [shift(sums[turn].astype(BF), axis, -turn) for turn in range(1, ring)]
        done.append(total(sums[0], *arrived).astype(BF))
    return done


def body(
    tokens,
    grad_out,
    gate_weight,
    up_weight,
    down_weight,
    gate_block_pairs,
    up_blocks,
    down_blocks,
    column_order,
):
    n_mp, n_dp = lax.axis_size(MP), lax.axis_size(DP)
    member, shard = lax.axis_index(MP), lax.axis_index(DP)
    x, y, z, core = (lax.axis_index(a) for a in ("x", "y", "z", "c"))
    ring = lax.axis_size("x")
    held = gate_weight.shape[0]
    quota = held // n_mp
    slab = BS // n_dp
    per = tokens.shape[1] // BS
    n_rows = per * n_mp
    owned = column_order.shape[0] // n_mp
    count = 3 * held
    tok = tokens.shape[0]

    x_all = lax.all_gather(jnp.stack([tokens, grad_out]), MP, axis=0, tiled=False)

    slabs = jnp.stack(
        [
            lax.dynamic_slice_in_dim(w, shard * slab, slab, 1).reshape(n_mp, quota, slab, BS)
            for w in (gate_weight, up_weight, down_weight)
        ],
        axis=1,
    )
    mine = lax.all_to_all(slabs, MP, split_axis=0, concat_axis=0, tiled=True)
    weights = spread(mine.reshape(count, slab, BS))

    tables = jnp.stack([gate_block_pairs, up_blocks, down_blocks])
    tables = tables.reshape(3, n_mp, n_mp, quota, 2)
    tables = lax.dynamic_index_in_dim(tables, member, 2, keepdims=False).transpose(1, 0, 2, 3)
    is_down = (jnp.arange(3) == 2)[None, :, None]
    rows = jnp.where(is_down, tables[..., 1], tables[..., 0]).reshape(count)
    names = jnp.where(is_down, tables[..., 0], tables[..., 1]).reshape(count)
    near, far = (x + ring - rows // (per * ring)) % ring, (z + ring - rows // per % ring) % ring
    hops = (near * ring + far) * per + rows % per
    own_cols = lax.dynamic_slice_in_dim(column_order, member * owned, owned, 0)
    cols = jnp.sum(
        jnp.where(names[:, None] == own_cols[None, :], jnp.arange(owned, dtype=jnp.int32), 0),
        axis=1,
    )
    slots = jnp.stack(
        [(y + hop + ring) % ring * 2 + c for hop in (0, -1, 1, 2) for c in (core, 1 - core)]
    ).astype(jnp.int32)

    act_shape = (3, owned, tok, BS)
    x_shape = (n_mp, tok, per * BS)
    grad_shape = (n_dp, count, slab, BS)
    whole = pltpu.VMEM((count, n_dp, slab, BS), BF)
    sizes = dict(per=per, quota=quota, count=len(weights))

    act, hidden_own, grads = pl.pallas_call(
        functools.partial(owner_kernel, owned=owned, **sizes),
        out_shape=[jax.ShapeDtypeStruct(act_shape, BF), jax.ShapeDtypeStruct((tok, owned * BS), BF)]
        + [jax.ShapeDtypeStruct(grad_shape, BF)],
        in_specs=[SMEM] * 3 + [ANY] * (1 + len(weights)),
        out_specs=[VMEM] * 2 + [ANY],
        scratch_shapes=[
            pltpu.VMEM(x_shape, BF),
            pltpu.VMEM(x_shape, BF),
            pltpu.VMEM((n_rows, BS, tok), BF),
            whole,
            pltpu.VMEM(act_shape, F32),
            pltpu.VMEM((owned, BS, tok), BF),
            pltpu.VMEM(grad_shape, BF),
            pltpu.SemaphoreType.DMA((len(weights) + 12,)),
        ],
        name="owner",
    )(rows, cols, slots, x_all, *weights)
    grads = lax.psum_scatter(grads, DP, scatter_dimension=0, tiled=True)

    part_shape = (ring, tok, per * BS)
    by_share = [w.reshape(-1, 3, quota, slab, BS) for w in weights]

    def parts_of(projections):
        return pl.pallas_call(
            functools.partial(parts_kernel, ring=ring, projections=projections, **sizes),
            out_shape=[jax.ShapeDtypeStruct(part_shape, BF)] * ring,
            in_specs=[SMEM] * 3 + [VMEM] + [ANY] * len(weights),
            out_specs=[ANY] * ring,
            scratch_shapes=[
                pltpu.VMEM((n_rows, tok, BS), F32),
                pltpu.VMEM((n_mp, len(projections), quota, n_dp, slab, BS), BF),
                pltpu.VMEM((ring,) + part_shape, BF),
                pltpu.SemaphoreType.DMA((len(weights) + ring,)),
            ],
        )(hops, cols, slots, act, *by_share)

    out_parts, in_parts = parts_of((2,)), parts_of((0, 1))
    output, input_grad = collect(out_parts, in_parts)
    grads = grads.reshape(n_mp, 3, quota, slab, BS)
    grads = lax.all_to_all(grads, MP, split_axis=0, concat_axis=0, tiled=True)
    gate_grad, up_grad, down_grad = (grads[:, p].reshape(held, slab, BS) for p in range(3))
    return (hidden_own, output, input_grad, gate_grad, up_grad, down_grad)


def solution(mesh):
    mesh = Mesh(mesh.devices.reshape(4, 2, 4, 4), DP + MP)
    wide_spec, block_spec, grad_spec = P(DP, MP), P(MP, None, None), P(MP, DP, None)
    return jax.shard_map(
        body,
        mesh=mesh,
        in_specs=(wide_spec,) * 2 + (block_spec,) * 3 + (P(),) * 4,
        out_specs=(wide_spec,) * 3 + (grad_spec,) * 3,
        check_vma=False,
    )
```

```python
import functools

import jax
import jax.numpy as jnp
from jax import lax
from jax.experimental import pallas as pl
from jax.experimental.pallas import tpu as pltpu
from jax.sharding import Mesh, PartitionSpec as P

BS = 128
UNROLL = 4
MP = ("x", "z")
DP = ("y", "c")
BF = jnp.bfloat16
F32 = jnp.float32
SMEM = pl.BlockSpec(memory_space=pltpu.SMEM)
ANY = pl.BlockSpec(memory_space=pl.ANY)
VMEM = pl.BlockSpec(memory_space=pltpu.VMEM)


def dot(a, b):
    return lax.dot_general(a, b, (((1,), (0,)), ((), ())), preferred_element_type=F32)


def dot_t(a, b):
    return lax.dot_general(a, b, (((1,), (1,)), ((), ())), preferred_element_type=F32)


def start_all(pairs, sems, first):
    copies = [pltpu.make_async_copy(a, b, sems.at[first + i]) for i, (a, b) in enumerate(pairs)]
    for copy in copies:
        copy.start()
    return copies


def wait_all(copies):
    for copy in copies:
        copy.wait()


def piece_pairs(slots, pieces, whole):
    half = whole.shape[0] // 2
    at = lambda part, i: whole.at[(part,) + (slice(None),) * (len(whole.shape) - 4) + (slots[i],)]
    own = [(pieces[i], at(slice(None), i)) for i in range(2)]
    early = [(pieces[2 * i - 2], at(slice(half), i)) for i in range(2, 8)]
    late = [(pieces[2 * i - 1], at(slice(half, 2 * half), i)) for i in range(2, 8)]
    return own, early, late


def wide(ref, block, per):
    lane = pl.multiple_of((block & (per - 1)) * BS, BS)
    return ref[block >> (per.bit_length() - 1), :, pl.ds(lane, BS)]


def each_block(low, high, rows, cols, quota, projections, visit):
    def share(i, carry):
        for proj in projections:
            for b in range(quota):
                k = (i * 3 + proj) * quota + b
                visit((i, proj, b), k, rows[k], cols[k])
        return carry

    lax.fori_loop(low, high, share, 0, unroll=UNROLL)


def send_parts(acc, stage, outs, sems, first, per, by_near):
    ring, copies = len(outs), []
    for hop in list(range(1, ring)) + [0]:
        for turn in range(ring):
            near = hop * ring + turn if by_near else turn * ring + hop
            for q in range(per):
                stage[hop, turn, :, q * BS : (q + 1) * BS] = acc[near * per + q].astype(BF)
        copies += start_all([(stage.at[hop], outs[hop])], sems, first + hop)
    return copies


def owner_kernel(rows, hops, cols, slots, x_all, *refs, ring, per, quota, owned, count):
    pieces, refs = refs[:count], refs[count:]
    act_ref, own_ref, result = refs[:3]
    outs, refs = refs[3 : 3 + ring], refs[3 + ring :]
    tok, cot, flipped, whole, acc, out_acc, flipped_hidden, stage, out_stage, sems = refs
    shares, members = whole.shape[0] // (3 * quota), tok.shape[0]
    half, line = whole.shape[0] // 2, members // 4

    def quarters(which, ref):
        return [(x_all.at[i * line : (i + 1) * line, which], ref.at[i * line : (i + 1) * line]) for i in range(4)]

    own, early, late = piece_pairs(slots, pieces, whole)
    tok_copies = start_all(quarters(0, tok), sems, 0)
    early_copies = start_all(own + early + quarters(1, cot), sems, 4)
    late_copies = start_all(late, sems, 4 + len(early_copies))
    acc[...] = jnp.zeros_like(acc)
    out_acc[...] = jnp.zeros_like(out_acc)

    index = lambda d: lax.broadcasted_iota(jnp.int32, (BS, BS), d)
    unit = jnp.where(index(0) == index(1), 1.0, 0.0).astype(BF)

    def add(at, k, r, c):
        proj, w = at[1], whole[k].reshape(BS, BS)
        if proj == 0:
            x = tok[at[0], :, at[2] * BS : (at[2] + 1) * BS]
            flipped[at[0] * per + at[2]] = x.T
        if proj < 2:
            acc[proj, c] += dot(wide(tok, r, per), w)
        else:
            acc[proj, c] += dot_t(wide(cot, r, per), w)

    wait_all(tok_copies + early_copies)
    each_block(0, shares // 2, rows, cols, quota, range(3), add)
    wait_all(late_copies)
    each_block(shares // 2, shares, rows, cols, quota, range(3), add)

    for c in range(owned):
        gate, up, grad = acc[0, c], acc[1, c], acc[2, c]
        s = jax.nn.sigmoid(gate)
        silu = gate * s
        hidden = (silu * up).astype(BF)
        act_ref[0, c] = hidden
        own_ref[:, c * BS : (c + 1) * BS] = hidden
        act_ref[1, c] = (grad * up * s * (1.0 + gate * (1.0 - s))).astype(BF)
        act_ref[2, c] = (grad * silu).astype(BF)
        flipped_hidden[c] = dot_t(unit, hidden).astype(BF)

    def down(at, k, r, c):
        out_acc[r] += dot(act_ref[0, c], whole[k].reshape(BS, BS))

    each_block(0, shares, hops, cols, quota, (2,), down)
    first = 4 + len(early_copies) + len(late_copies)
    copies = send_parts(out_acc, out_stage, outs, sems, first, per, True)

    def outer(at, k, r, c):
        if at[1] < 2:
            g = dot(flipped[r], act_ref[1 + at[1], c])
        else:
            g = dot(flipped_hidden[c], wide(cot, r, per))
        stage[:, k] = g.astype(BF).reshape(stage.shape[0], -1, BS)

    for part in range(4):
        each_block(part * shares // 4, (part + 1) * shares // 4, rows, cols, quota, range(3), outer)
        at = pl.ds(part * half // 2, half // 2)
        copies += start_all(
            [(stage.at[:, at], result.at[:, at])],
            sems,
            first + ring + part,
        )
    wait_all(copies)


def parts_kernel(rows, cols, slots, act_ref, *refs, ring, per, quota, count, projections):
    pieces, outs = refs[:count], refs[count : count + ring]
    acc, whole, stage, sems = refs[count + ring :]
    shares = whole.shape[0]
    some = slice(projections[0], projections[-1] + 1)
    own, early, late = [
        [(piece.at[:, some], place) for piece, place in pairs]
        for pairs in piece_pairs(slots, pieces, whole)
    ]
    early_copies = start_all(own + early, sems, 0)
    late_copies = start_all(late, sems, len(early_copies))
    acc[...] = jnp.zeros_like(acc)

    def add(at, k, r, c):
        w = whole[at[0], at[1] - projections[0], at[2]].reshape(BS, BS)
        if at[1] < 2:
            acc[r] += dot_t(act_ref[1 + at[1], c], w)
        else:
            acc[r] += dot(act_ref[0, c], w)

    wait_all(early_copies)
    each_block(0, shares // 2, rows, cols, quota, projections, add)
    wait_all(late_copies)
    each_block(shares // 2, shares, rows, cols, quota, projections, add)

    wait_all(send_parts(acc, stage, outs, sems, count, per, projections[0] == 2))


def pair_kernel(a, b, out, sems):
    wait_all(start_all([(a, out.at[0]), (b, out.at[1])], sems, 0))


def shift(value, axis, hop):
    size = lax.axis_size(axis)
    return lax.ppermute(value, axis, [(i, (i + hop) % size) for i in range(size)])


def total(*terms):
    return sum(t.astype(F32) for t in terms)


def spread(mine):
    half = mine.shape[0] // 2
    parts = mine[:half], mine[half:]
    up, down = [None] * 2, [None] * 2
    up[0], down[1] = shift(parts[0], "y", 1), shift(parts[1], "y", -1)
    up[1], down[0] = shift(parts[1], "y", 1), shift(parts[0], "y", -1)
    far = [shift(up[0], "y", 1), shift(down[1], "y", -1)]
    swap = lambda value: shift(value, "c", 1)
    pieces = [mine, swap(mine)]
    for pair in (up, down, far):
        pieces += pair + [swap(v) for v in pair]
    return pieces


def collect(outs, grads):
    ring = len(outs)
    first = [[p[0]] + [shift(p[h], a, -h) for h in range(1, ring)] for p, a in ((outs, "x"), (grads, "z"))]
    done = []
    for terms, axis in zip(first, ("z", "x")):
        sums = [total(*[t[turn] for t in terms]) for turn in range(ring)]
        arrived = [shift(sums[turn].astype(BF), axis, -turn) for turn in range(1, ring)]
        done.append(total(sums[0], *arrived).astype(BF))
    return done


def body(
    tokens,
    grad_out,
    gate_weight,
    up_weight,
    down_weight,
    gate_block_pairs,
    up_blocks,
    down_blocks,
    column_order,
):
    n_mp, n_dp = lax.axis_size(MP), lax.axis_size(DP)
    member, shard = lax.axis_index(MP), lax.axis_index(DP)
    x, y, z, core = (lax.axis_index(a) for a in ("x", "y", "z", "c"))
    ring = lax.axis_size("x")
    held = gate_weight.shape[0]
    quota = held // n_mp
    slab = BS // n_dp
    per = tokens.shape[1] // BS
    n_rows = per * n_mp
    owned = column_order.shape[0] // n_mp
    count = 3 * held
    tok = tokens.shape[0]

    pair = pl.pallas_call(
        pair_kernel,
        out_shape=jax.ShapeDtypeStruct((2,) + tokens.shape, BF),
        in_specs=[ANY] * 2,
        out_specs=ANY,
        scratch_shapes=[pltpu.SemaphoreType.DMA((2,))],
        name="pair",
    )(tokens, grad_out)
    x_all = lax.all_gather(pair, MP, axis=0, tiled=False)

    slabs = jnp.stack(
        [
            lax.dynamic_slice_in_dim(w, shard * slab, slab, 1).reshape(n_mp, quota, slab, BS)
            for w in (gate_weight, up_weight, down_weight)
        ],
        axis=1,
    )
    mine = lax.all_to_all(slabs, MP, split_axis=0, concat_axis=0, tiled=True)
    weights = spread(mine.reshape(count, slab, BS))

    tables = jnp.stack([gate_block_pairs, up_blocks, down_blocks])
    tables = tables.reshape(3, n_mp, n_mp, quota, 2)
    tables = lax.dynamic_index_in_dim(tables, member, 2, keepdims=False).transpose(1, 0, 2, 3)
    is_down = (jnp.arange(3) == 2)[None, :, None]
    rows = jnp.where(is_down, tables[..., 1], tables[..., 0]).reshape(count)
    names = jnp.where(is_down, tables[..., 0], tables[..., 1]).reshape(count)
    near, far = (x + ring - rows // (per * ring)) % ring, (z + ring - rows // per % ring) % ring
    hops = (near * ring + far) * per + rows % per
    own_cols = lax.dynamic_slice_in_dim(column_order, member * owned, owned, 0)
    cols = jnp.sum(
        jnp.where(names[:, None] == own_cols[None, :], jnp.arange(owned, dtype=jnp.int32), 0),
        axis=1,
    )
    slots = jnp.stack(
        [(y + hop + ring) % ring * 2 + c for hop in (0, -1, 1, 2) for c in (core, 1 - core)]
    ).astype(jnp.int32)

    act_shape = (3, owned, tok, BS)
    x_shape = (n_mp, tok, per * BS)
    grad_shape = (n_dp, count, slab, BS)
    whole = pltpu.VMEM((count, n_dp, slab, BS), BF)
    sizes = dict(ring=ring, per=per, quota=quota, count=len(weights))

    part_shape = (ring, tok, per * BS)
    act, hidden_own, grads, *out_parts = pl.pallas_call(
        functools.partial(owner_kernel, owned=owned, **sizes),
        out_shape=[jax.ShapeDtypeStruct(act_shape, BF), jax.ShapeDtypeStruct((tok, owned * BS), BF)]
        + [jax.ShapeDtypeStruct(grad_shape, BF)]
        + [jax.ShapeDtypeStruct(part_shape, BF)] * ring,
        in_specs=[SMEM] * 4 + [ANY] * (1 + len(weights)),
        out_specs=[VMEM] * 2 + [ANY] * (1 + ring),
        scratch_shapes=[
            pltpu.VMEM(x_shape, BF),
            pltpu.VMEM(x_shape, BF),
            pltpu.VMEM((n_rows, BS, tok), BF),
            whole,
            pltpu.VMEM(act_shape, F32),
            pltpu.VMEM((n_rows, tok, BS), F32),
            pltpu.VMEM((owned, BS, tok), BF),
            pltpu.VMEM(grad_shape, BF),
            pltpu.VMEM((ring,) + part_shape, BF),
            pltpu.SemaphoreType.DMA((len(weights) + 12 + ring,)),
        ],
        name="owner",
    )(rows, hops, cols, slots, x_all, *weights)
    grads = lax.psum_scatter(grads, DP, scatter_dimension=0, tiled=True)

    by_share = [w.reshape(-1, 3, quota, slab, BS) for w in weights]

    def parts_of(projections):
        return pl.pallas_call(
            functools.partial(parts_kernel, projections=projections, **sizes),
            out_shape=[jax.ShapeDtypeStruct(part_shape, BF)] * ring,
            in_specs=[SMEM] * 3 + [VMEM] + [ANY] * len(weights),
            out_specs=[ANY] * ring,
            scratch_shapes=[
                pltpu.VMEM((n_rows, tok, BS), F32),
                pltpu.VMEM((n_mp, len(projections), quota, n_dp, slab, BS), BF),
                pltpu.VMEM((ring,) + part_shape, BF),
                pltpu.SemaphoreType.DMA((len(weights) + ring,)),
            ],
        )(hops, cols, slots, act, *by_share)

    in_parts = parts_of((0, 1))
    output, input_grad = collect(out_parts, in_parts)
    grads = grads.reshape(n_mp, 3, quota, slab, BS)
    grads = lax.all_to_all(grads, MP, split_axis=0, concat_axis=0, tiled=True)
    gate_grad, up_grad, down_grad = (grads[:, p].reshape(held, slab, BS) for p in range(3))
    return (hidden_own, output, input_grad, gate_grad, up_grad, down_grad)


def solution(mesh):
    mesh = Mesh(mesh.devices.reshape(4, 2, 4, 4), DP + MP)
    wide_spec, block_spec, grad_spec = P(DP, MP), P(MP, None, None), P(MP, DP, None)
    return jax.shard_map(
        body,
        mesh=mesh,
        in_specs=(wide_spec,) * 2 + (block_spec,) * 3 + (P(),) * 4,
        out_specs=(wide_spec,) * 3 + (grad_spec,) * 3,
        check_vma=False,
    )
```

```python
import functools

import jax
import jax.numpy as jnp
from jax import lax
from jax.experimental import pallas as pl
from jax.experimental.pallas import tpu as pltpu
from jax.sharding import Mesh, PartitionSpec as P

BS = 128
UNROLL = 4
MP = ("x", "z")
DP = ("y", "c")
BF = jnp.bfloat16
F32 = jnp.float32
SMEM = pl.BlockSpec(memory_space=pltpu.SMEM)
ANY = pl.BlockSpec(memory_space=pl.ANY)
VMEM = pl.BlockSpec(memory_space=pltpu.VMEM)


def dot(a, b):
    return lax.dot_general(a, b, (((1,), (0,)), ((), ())), preferred_element_type=F32)


def dot_t(a, b):
    return lax.dot_general(a, b, (((1,), (1,)), ((), ())), preferred_element_type=F32)


def start_all(pairs, sems, first):
    copies = [pltpu.make_async_copy(a, b, sems.at[first + i]) for i, (a, b) in enumerate(pairs)]
    for copy in copies:
        copy.start()
    return copies


def wait_all(copies):
    for copy in copies:
        copy.wait()


def piece_pairs(slots, pieces, whole):
    half = whole.shape[0] // 2
    at = lambda part, i: whole.at[(part,) + (slice(None),) * (len(whole.shape) - 4) + (slots[i],)]
    own = [(pieces[i], at(slice(None), i)) for i in range(2)]
    early = [(pieces[2 * i - 2], at(slice(half), i)) for i in range(2, 8)]
    late = [(pieces[2 * i - 1], at(slice(half, 2 * half), i)) for i in range(2, 8)]
    return own, early, late


def wide(ref, block, per):
    lane = pl.multiple_of((block & (per - 1)) * BS, BS)
    return ref[block >> (per.bit_length() - 1), :, pl.ds(lane, BS)]


def each_block(low, high, rows, cols, quota, projections, visit):
    def share(i, carry):
        for proj in projections:
            for b in range(quota):
                k = (i * 3 + proj) * quota + b
                visit((i, proj, b), k, rows[k], cols[k])
        return carry

    lax.fori_loop(low, high, share, 0, unroll=UNROLL)


def send_parts(acc, stage, outs, sems, first, per, by_near):
    ring, copies = len(outs), []
    for hop in list(range(1, ring)) + [0]:
        for turn in range(ring):
            near = hop * ring + turn if by_near else turn * ring + hop
            for q in range(per):
                stage[hop, turn, :, q * BS : (q + 1) * BS] = acc[near * per + q].astype(BF)
        copies += start_all([(stage.at[hop], outs[hop])], sems, first + hop)
    return copies


def owner_kernel(rows, hops, cols, slots, x_all, *refs, ring, per, quota, owned, count):
    pieces, refs = refs[:count], refs[count:]
    act_ref, own_ref, result = refs[:3]
    outs, refs = refs[3 : 3 + ring], refs[3 + ring :]
    tok, cot, flipped, whole, acc, out_acc, flipped_hidden, stage, out_stage, sems = refs
    shares, members = whole.shape[0] // (3 * quota), tok.shape[0]
    half, line = whole.shape[0] // 2, members // 4

    def quarters(which, ref):
        return [(x_all.at[i * line : (i + 1) * line, which], ref.at[i * line : (i + 1) * line]) for i in range(4)]

    own, early, late = piece_pairs(slots, pieces, whole)
    tok_copies = start_all(quarters(0, tok), sems, 0)
    early_copies = start_all(own + early + quarters(1, cot), sems, 4)
    late_copies = start_all(late, sems, 4 + len(early_copies))
    acc[...] = jnp.zeros_like(acc)
    out_acc[...] = jnp.zeros_like(out_acc)

    index = lambda d: lax.broadcasted_iota(jnp.int32, (BS, BS), d)
    unit = jnp.where(index(0) == index(1), 1.0, 0.0).astype(BF)

    def add(at, k, r, c):
        proj, w = at[1], whole[k].reshape(BS, BS)
        if proj == 0:
            x = tok[at[0], :, at[2] * BS : (at[2] + 1) * BS]
            flipped[at[0] * per + at[2]] = x.T
        if proj < 2:
            acc[proj, c] += dot(wide(tok, r, per), w)
        else:
            acc[proj, c] += dot_t(wide(cot, r, per), w)

    wait_all(tok_copies + early_copies)
    each_block(0, shares // 2, rows, cols, quota, range(3), add)
    wait_all(late_copies)
    each_block(shares // 2, shares, rows, cols, quota, range(3), add)

    for c in range(owned):
        gate, up, grad = acc[0, c], acc[1, c], acc[2, c]
        s = jax.nn.sigmoid(gate)
        silu = gate * s
        hidden = (silu * up).astype(BF)
        act_ref[0, c] = hidden
        own_ref[:, c * BS : (c + 1) * BS] = hidden
        act_ref[1, c] = (grad * up * s * (1.0 + gate * (1.0 - s))).astype(BF)
        act_ref[2, c] = (grad * silu).astype(BF)
        flipped_hidden[c] = dot_t(unit, hidden).astype(BF)

    def down(at, k, r, c):
        out_acc[r] += dot(act_ref[0, c], whole[k].reshape(BS, BS))

    each_block(0, shares, hops, cols, quota, (2,), down)
    first = 4 + len(early_copies) + len(late_copies)
    copies = send_parts(out_acc, out_stage, outs, sems, first, per, True)

    def outer(at, k, r, c):
        if at[1] < 2:
            g = dot(flipped[r], act_ref[1 + at[1], c])
        else:
            g = dot(flipped_hidden[c], wide(cot, r, per))
        stage[:, k] = g.astype(BF).reshape(stage.shape[0], -1, BS)

    for part in range(4):
        each_block(part * shares // 4, (part + 1) * shares // 4, rows, cols, quota, range(3), outer)
        at = pl.ds(part * half // 2, half // 2)
        copies += start_all(
            [(stage.at[:, at], result.at[:, at])],
            sems,
            first + ring + part,
        )
    wait_all(copies)


def parts_kernel(rows, cols, slots, act_ref, *refs, ring, per, quota, count, projections):
    pieces, outs = refs[:count], refs[count : count + ring]
    acc, whole, stage, sems = refs[count + ring :]
    shares = whole.shape[0]
    some = slice(projections[0], projections[-1] + 1)
    own, early, late = [
        [(piece.at[:, some], place) for piece, place in pairs]
        for pairs in piece_pairs(slots, pieces, whole)
    ]
    early_copies = start_all(own + early, sems, 0)
    late_copies = start_all(late, sems, len(early_copies))
    acc[...] = jnp.zeros_like(acc)

    def add(at, k, r, c):
        w = whole[at[0], at[1] - projections[0], at[2]].reshape(BS, BS)
        if at[1] < 2:
            acc[r] += dot_t(act_ref[1 + at[1], c], w)
        else:
            acc[r] += dot(act_ref[0, c], w)

    wait_all(early_copies)
    each_block(0, shares // 2, rows, cols, quota, projections, add)
    wait_all(late_copies)
    each_block(shares // 2, shares, rows, cols, quota, projections, add)

    wait_all(send_parts(acc, stage, outs, sems, count, per, projections[0] == 2))


def shift(value, axis, hop):
    size = lax.axis_size(axis)
    return lax.ppermute(value, axis, [(i, (i + hop) % size) for i in range(size)])


def total(*terms):
    return sum(t.astype(F32) for t in terms)


def spread(mine):
    half = mine.shape[0] // 2
    parts = mine[:half], mine[half:]
    up, down = [None] * 2, [None] * 2
    up[0], down[1] = shift(parts[0], "y", 1), shift(parts[1], "y", -1)
    up[1], down[0] = shift(parts[1], "y", 1), shift(parts[0], "y", -1)
    far = [shift(up[0], "y", 1), shift(down[1], "y", -1)]
    swap = lambda value: shift(value, "c", 1)
    pieces = [mine, swap(mine)]
    for pair in (up, down, far):
        pieces += pair + [swap(v) for v in pair]
    return pieces


def collect(outs, grads, other):
    ring = len(outs)
    first = [[p[0]] + [shift(p[h], a, -h) for h in range(1, ring)] for p, a in ((outs, "x"), (grads, "z"))]
    sums = [[total(*[t[turn] for t in terms]) for turn in range(ring)] for terms in first]
    moved = [[v.astype(BF) for v in s[1:]] for s in sums]
    moved[1], other = lax.optimization_barrier((moved[1], other))
    done = []
    for s, m, axis in zip(sums, moved, ("z", "x")):
        arrived = [shift(m[turn - 1], axis, -turn) for turn in range(1, ring)]
        done.append(total(s[0], *arrived).astype(BF))
    return done, other


def body(
    tokens,
    grad_out,
    gate_weight,
    up_weight,
    down_weight,
    gate_block_pairs,
    up_blocks,
    down_blocks,
    column_order,
):
    n_mp, n_dp = lax.axis_size(MP), lax.axis_size(DP)
    member, shard = lax.axis_index(MP), lax.axis_index(DP)
    x, y, z, core = (lax.axis_index(a) for a in ("x", "y", "z", "c"))
    ring = lax.axis_size("x")
    held = gate_weight.shape[0]
    quota = held // n_mp
    slab = BS // n_dp
    per = tokens.shape[1] // BS
    n_rows = per * n_mp
    owned = column_order.shape[0] // n_mp
    count = 3 * held
    tok = tokens.shape[0]

    x_all = lax.all_gather(jnp.stack([tokens, grad_out]), MP, axis=0, tiled=False)

    slabs = jnp.stack(
        [
            lax.dynamic_slice_in_dim(w, shard * slab, slab, 1).reshape(n_mp, quota, slab, BS)
            for w in (gate_weight, up_weight, down_weight)
        ],
        axis=1,
    )
    mine = lax.all_to_all(slabs, MP, split_axis=0, concat_axis=0, tiled=True)
    weights = spread(mine.reshape(count, slab, BS))

    tables = jnp.stack([gate_block_pairs, up_blocks, down_blocks])
    tables = tables.reshape(3, n_mp, n_mp, quota, 2)
    tables = lax.dynamic_index_in_dim(tables, member, 2, keepdims=False).transpose(1, 0, 2, 3)
    is_down = (jnp.arange(3) == 2)[None, :, None]
    rows = jnp.where(is_down, tables[..., 1], tables[..., 0]).reshape(count)
    names = jnp.where(is_down, tables[..., 0], tables[..., 1]).reshape(count)
    near, far = (x + ring - rows // (per * ring)) % ring, (z + ring - rows // per % ring) % ring
    hops = (near * ring + far) * per + rows % per
    own_cols = lax.dynamic_slice_in_dim(column_order, member * owned, owned, 0)
    cols = jnp.sum(
        jnp.where(names[:, None] == own_cols[None, :], jnp.arange(owned, dtype=jnp.int32), 0),
        axis=1,
    )
    slots = jnp.stack(
        [(y + hop + ring) % ring * 2 + c for hop in (0, -1, 1, 2) for c in (core, 1 - core)]
    ).astype(jnp.int32)

    act_shape = (3, owned, tok, BS)
    x_shape = (n_mp, tok, per * BS)
    grad_shape = (n_dp, count, slab, BS)
    whole = pltpu.VMEM((count, n_dp, slab, BS), BF)
    sizes = dict(ring=ring, per=per, quota=quota, count=len(weights))

    part_shape = (ring, tok, per * BS)
    act, hidden_own, grads, *out_parts = pl.pallas_call(
        functools.partial(owner_kernel, owned=owned, **sizes),
        out_shape=[jax.ShapeDtypeStruct(act_shape, BF), jax.ShapeDtypeStruct((tok, owned * BS), BF)]
        + [jax.ShapeDtypeStruct(grad_shape, BF)]
        + [jax.ShapeDtypeStruct(part_shape, BF)] * ring,
        in_specs=[SMEM] * 4 + [ANY] * (1 + len(weights)),
        out_specs=[VMEM] * 2 + [ANY] * (1 + ring),
        scratch_shapes=[
            pltpu.VMEM(x_shape, BF),
            pltpu.VMEM(x_shape, BF),
            pltpu.VMEM((n_rows, BS, tok), BF),
            whole,
            pltpu.VMEM(act_shape, F32),
            pltpu.VMEM((n_rows, tok, BS), F32),
            pltpu.VMEM((owned, BS, tok), BF),
            pltpu.VMEM(grad_shape, BF),
            pltpu.VMEM((ring,) + part_shape, BF),
            pltpu.SemaphoreType.DMA((len(weights) + 12 + ring,)),
        ],
        name="owner",
    )(rows, hops, cols, slots, x_all, *weights)
    grads = lax.psum_scatter(grads, DP, scatter_dimension=0, tiled=True)

    by_share = [w.reshape(-1, 3, quota, slab, BS) for w in weights]

    def parts_of(projections):
        return pl.pallas_call(
            functools.partial(parts_kernel, projections=projections, **sizes),
            out_shape=[jax.ShapeDtypeStruct(part_shape, BF)] * ring,
            in_specs=[SMEM] * 3 + [VMEM] + [ANY] * len(weights),
            out_specs=[ANY] * ring,
            scratch_shapes=[
                pltpu.VMEM((n_rows, tok, BS), F32),
                pltpu.VMEM((n_mp, len(projections), quota, n_dp, slab, BS), BF),
                pltpu.VMEM((ring,) + part_shape, BF),
                pltpu.SemaphoreType.DMA((len(weights) + ring,)),
            ],
        )(hops, cols, slots, act, *by_share)

    in_parts = parts_of((0, 1))
    (output, input_grad), grads = collect(out_parts, in_parts, grads)
    grads = grads.reshape(n_mp, 3, quota, slab, BS)
    grads = lax.all_to_all(grads, MP, split_axis=0, concat_axis=0, tiled=True)
    gate_grad, up_grad, down_grad = (grads[:, p].reshape(held, slab, BS) for p in range(3))
    return (hidden_own, output, input_grad, gate_grad, up_grad, down_grad)


def solution(mesh):
    mesh = Mesh(mesh.devices.reshape(4, 2, 4, 4), DP + MP)
    wide_spec, block_spec, grad_spec = P(DP, MP), P(MP, None, None), P(MP, DP, None)
    return jax.shard_map(
        body,
        mesh=mesh,
        in_specs=(wide_spec,) * 2 + (block_spec,) * 3 + (P(),) * 4,
        out_specs=(wide_spec,) * 3 + (grad_spec,) * 3,
        check_vma=False,
    )
```

```python
import functools

import jax
import jax.numpy as jnp
from jax import lax
from jax.experimental import pallas as pl
from jax.experimental.pallas import tpu as pltpu
from jax.sharding import Mesh, PartitionSpec as P

BS = 128
UNROLL = 4
MP = ("x", "z")
DP = ("y", "c")
BF = jnp.bfloat16
F32 = jnp.float32
SMEM = pl.BlockSpec(memory_space=pltpu.SMEM)
ANY = pl.BlockSpec(memory_space=pl.ANY)
VMEM = pl.BlockSpec(memory_space=pltpu.VMEM)


def dot(a, b):
    return lax.dot_general(a, b, (((1,), (0,)), ((), ())), preferred_element_type=F32)


def dot_t(a, b):
    return lax.dot_general(a, b, (((1,), (1,)), ((), ())), preferred_element_type=F32)


def start_all(pairs, sems, first):
    copies = [pltpu.make_async_copy(a, b, sems.at[first + i]) for i, (a, b) in enumerate(pairs)]
    for copy in copies:
        copy.start()
    return copies


def wait_all(copies):
    for copy in copies:
        copy.wait()


def piece_pairs(slots, pieces, whole):
    half = whole.shape[0] // 2
    at = lambda part, i: whole.at[(part,) + (slice(None),) * (len(whole.shape) - 4) + (slots[i],)]
    own = [(pieces[i], at(slice(None), i)) for i in range(2)]
    early = [(pieces[2 * i - 2], at(slice(half), i)) for i in range(2, 8)]
    late = [(pieces[2 * i - 1], at(slice(half, 2 * half), i)) for i in range(2, 8)]
    return own, early, late


def wide(ref, block, per):
    lane = pl.multiple_of((block & (per - 1)) * BS, BS)
    return ref[block >> (per.bit_length() - 1), :, pl.ds(lane, BS)]


def each_block(low, high, rows, cols, quota, projections, visit):
    def share(i, carry):
        for proj in projections:
            for b in range(quota):
                k = (i * 3 + proj) * quota + b
                visit((i, proj, b), k, rows[k], cols[k])
        return carry

    lax.fori_loop(low, high, share, 0, unroll=UNROLL)


def send_parts(acc, stage, outs, sems, first, per, by_near):
    ring, copies = len(outs), []
    for hop in list(range(1, ring)) + [0]:
        for turn in range(ring):
            near = hop * ring + turn if by_near else turn * ring + hop
            for q in range(per):
                stage[hop, turn, :, q * BS : (q + 1) * BS] = acc[near * per + q].astype(BF)
        copies += start_all([(stage.at[hop], outs[hop])], sems, first + hop)
    return copies


def owner_kernel(rows, hops, cols, slots, x_all, *refs, ring, per, quota, owned, count):
    pieces, refs = refs[:count], refs[count:]
    act_ref, own_ref, result = refs[:3]
    outs, refs = refs[3 : 3 + ring], refs[3 + ring :]
    tok, cot, flipped, whole, acc, out_acc, flipped_hidden, stage, out_stage, sems = refs
    shares, members = whole.shape[0] // (3 * quota), tok.shape[0]
    half, line = whole.shape[0] // 2, members // 4

    def quarters(which, ref):
        return [(x_all.at[i * line : (i + 1) * line, which], ref.at[i * line : (i + 1) * line]) for i in range(4)]

    own, early, late = piece_pairs(slots, pieces, whole)
    tok_copies = start_all(quarters(0, tok), sems, 0)
    early_copies = start_all(own + early + quarters(1, cot), sems, 4)
    late_copies = start_all(late, sems, 4 + len(early_copies))
    acc[...] = jnp.zeros_like(acc)
    out_acc[...] = jnp.zeros_like(out_acc)

    index = lambda d: lax.broadcasted_iota(jnp.int32, (BS, BS), d)
    unit = jnp.where(index(0) == index(1), 1.0, 0.0).astype(BF)

    def add(at, k, r, c):
        proj, w = at[1], whole[k].reshape(BS, BS)
        if proj == 0:
            x = tok[at[0], :, at[2] * BS : (at[2] + 1) * BS]
            flipped[at[0] * per + at[2]] = x.T
        if proj < 2:
            acc[proj, c] += dot(wide(tok, r, per), w)
        else:
            acc[proj, c] += dot_t(wide(cot, r, per), w)

    wait_all(tok_copies + early_copies)
    each_block(0, shares // 2, rows, cols, quota, range(3), add)
    wait_all(late_copies)
    each_block(shares // 2, shares, rows, cols, quota, range(3), add)

    for c in range(owned):
        gate, up, grad = acc[0, c], acc[1, c], acc[2, c]
        s = jax.nn.sigmoid(gate)
        silu = gate * s
        hidden = (silu * up).astype(BF)
        act_ref[0, c] = hidden
        own_ref[:, c * BS : (c + 1) * BS] = hidden
        act_ref[1, c] = (grad * up * s * (1.0 + gate * (1.0 - s))).astype(BF)
        act_ref[2, c] = (grad * silu).astype(BF)
        flipped_hidden[c] = dot_t(unit, hidden).astype(BF)

    def down(at, k, r, c):
        out_acc[r] += dot(act_ref[0, c], whole[k].reshape(BS, BS))

    each_block(0, shares, hops, cols, quota, (2,), down)
    first = 4 + len(early_copies) + len(late_copies)
    copies = send_parts(out_acc, out_stage, outs, sems, first, per, True)

    def outer(at, k, r, c):
        if at[1] < 2:
            g = dot(flipped[r], act_ref[1 + at[1], c])
        else:
            g = dot(flipped_hidden[c], wide(cot, r, per))
        stage[:, k] = g.astype(BF).reshape(stage.shape[0], -1, BS)

    for part in range(4):
        each_block(part * shares // 4, (part + 1) * shares // 4, rows, cols, quota, range(3), outer)
        at = pl.ds(part * half // 2, half // 2)
        copies += start_all(
            [(stage.at[:, at], result.at[:, at])],
            sems,
            first + ring + part,
        )
    wait_all(copies)


def parts_kernel(rows, cols, slots, act_ref, *refs, ring, per, quota, count, projections):
    pieces, outs = refs[:count], refs[count : count + ring]
    acc, whole, stage, sems = refs[count + ring :]
    shares = whole.shape[0]
    some = slice(projections[0], projections[-1] + 1)
    own, early, late = [
        [(piece.at[:, some], place) for piece, place in pairs]
        for pairs in piece_pairs(slots, pieces, whole)
    ]
    early_copies = start_all(own + early, sems, 0)
    late_copies = start_all(late, sems, len(early_copies))
    acc[...] = jnp.zeros_like(acc)

    def add(at, k, r, c):
        w = whole[at[0], at[1] - projections[0], at[2]].reshape(BS, BS)
        if at[1] < 2:
            acc[r] += dot_t(act_ref[1 + at[1], c], w)
        else:
            acc[r] += dot(act_ref[0, c], w)

    wait_all(early_copies)
    each_block(0, shares // 2, rows, cols, quota, projections, add)
    wait_all(late_copies)
    each_block(shares // 2, shares, rows, cols, quota, projections, add)

    wait_all(send_parts(acc, stage, outs, sems, count, per, projections[0] == 2))


def shift(value, axis, hop):
    size = lax.axis_size(axis)
    return lax.ppermute(value, axis, [(i, (i + hop) % size) for i in range(size)])


def total(*terms):
    return sum(t.astype(F32) for t in terms)


def spread(mine):
    half = mine.shape[0] // 2
    parts = mine[:half], mine[half:]
    up, down = [None] * 2, [None] * 2
    up[0], down[1] = shift(parts[0], "y", 1), shift(parts[1], "y", -1)
    up[1], down[0] = shift(parts[1], "y", 1), shift(parts[0], "y", -1)
    far = [shift(up[0], "y", 1), shift(down[1], "y", -1)]
    swap = lambda value: shift(value, "c", 1)
    pieces = [mine, swap(mine)]
    for pair in (up, down, far):
        pieces += pair + [swap(v) for v in pair]
    return pieces


def collect(outs, grads):
    ring = len(outs)
    first = []
    for p, a in ((outs, "x"), (grads, "z")):
        first.append([p[0]] + [shift(p[h], a, -h) for h in range(1, ring)])
    done = []
    for terms, axis in zip(first, ("z", "x")):
        sums = [total(*[t[turn] for t in terms]) for turn in range(ring)]
        arrived = [shift(sums[turn].astype(BF), axis, -turn) for turn in range(1, ring)]
        done.append(total(sums[0], *arrived).astype(BF))
    return done


def body(
    tokens,
    grad_out,
    gate_weight,
    up_weight,
    down_weight,
    gate_block_pairs,
    up_blocks,
    down_blocks,
    column_order,
):
    n_mp, n_dp = lax.axis_size(MP), lax.axis_size(DP)
    member, shard = lax.axis_index(MP), lax.axis_index(DP)
    x, y, z, core = (lax.axis_index(a) for a in ("x", "y", "z", "c"))
    ring = lax.axis_size("x")
    held = gate_weight.shape[0]
    quota = held // n_mp
    slab = BS // n_dp
    per = tokens.shape[1] // BS
    n_rows = per * n_mp
    owned = column_order.shape[0] // n_mp
    count = 3 * held
    tok = tokens.shape[0]

    x_all = lax.all_gather(jnp.stack([tokens, grad_out]), MP, axis=0, tiled=False)

    slabs = jnp.stack(
        [
            lax.dynamic_slice_in_dim(w, shard * slab, slab, 1).reshape(n_mp, quota, slab, BS)
            for w in (gate_weight, up_weight, down_weight)
        ],
        axis=1,
    )
    mine = lax.all_to_all(slabs, MP, split_axis=0, concat_axis=0, tiled=True)
    weights = spread(mine.reshape(count, slab, BS))

    tables = jnp.stack([gate_block_pairs, up_blocks, down_blocks])
    tables = tables.reshape(3, n_mp, n_mp, quota, 2)
    tables = lax.dynamic_index_in_dim(tables, member, 2, keepdims=False).transpose(1, 0, 2, 3)
    is_down = (jnp.arange(3) == 2)[None, :, None]
    rows = jnp.where(is_down, tables[..., 1], tables[..., 0]).reshape(count)
    names = jnp.where(is_down, tables[..., 0], tables[..., 1]).reshape(count)
    near, far = (x + ring - rows // (per * ring)) % ring, (z + ring - rows // per % ring) % ring
    hops = (near * ring + far) * per + rows % per
    own_cols = lax.dynamic_slice_in_dim(column_order, member * owned, owned, 0)
    cols = jnp.sum(
        jnp.where(names[:, None] == own_cols[None, :], jnp.arange(owned, dtype=jnp.int32), 0),
        axis=1,
    )
    slots = jnp.stack(
        [(y + hop + ring) % ring * 2 + c for hop in (0, -1, 1, 2) for c in (core, 1 - core)]
    ).astype(jnp.int32)

    act_shape = (3, owned, tok, BS)
    x_shape = (n_mp, tok, per * BS)
    grad_shape = (n_dp, count, slab, BS)
    whole = pltpu.VMEM((count, n_dp, slab, BS), BF)
    sizes = dict(ring=ring, per=per, quota=quota, count=len(weights))

    part_shape = (ring, tok, per * BS)
    act, hidden_own, grads, *out_parts = pl.pallas_call(
        functools.partial(owner_kernel, owned=owned, **sizes),
        out_shape=[jax.ShapeDtypeStruct(act_shape, BF), jax.ShapeDtypeStruct((tok, owned * BS), BF)]
        + [jax.ShapeDtypeStruct(grad_shape, BF)]
        + [jax.ShapeDtypeStruct(part_shape, BF)] * ring,
        in_specs=[SMEM] * 4 + [ANY] * (1 + len(weights)),
        out_specs=[VMEM] * 2 + [ANY] * (1 + ring),
        scratch_shapes=[
            pltpu.VMEM(x_shape, BF),
            pltpu.VMEM(x_shape, BF),
            pltpu.VMEM((n_rows, BS, tok), BF),
            whole,
            pltpu.VMEM(act_shape, F32),
            pltpu.VMEM((n_rows, tok, BS), F32),
            pltpu.VMEM((owned, BS, tok), BF),
            pltpu.VMEM(grad_shape, BF),
            pltpu.VMEM((ring,) + part_shape, BF),
            pltpu.SemaphoreType.DMA((len(weights) + 12 + ring,)),
        ],
        name="owner",
    )(rows, hops, cols, slots, x_all, *weights)
    grads = lax.psum_scatter(grads, DP, scatter_dimension=0, tiled=True)

    by_share = [w.reshape(-1, 3, quota, slab, BS) for w in weights]

    def parts_of(projections):
        return pl.pallas_call(
            functools.partial(parts_kernel, projections=projections, **sizes),
            out_shape=[jax.ShapeDtypeStruct(part_shape, BF)] * ring,
            in_specs=[SMEM] * 3 + [VMEM] + [ANY] * len(weights),
            out_specs=[ANY] * ring,
            scratch_shapes=[
                pltpu.VMEM((n_rows, tok, BS), F32),
                pltpu.VMEM((n_mp, len(projections), quota, n_dp, slab, BS), BF),
                pltpu.VMEM((ring,) + part_shape, BF),
                pltpu.SemaphoreType.DMA((len(weights) + ring,)),
            ],
        )(hops, cols, slots, act, *by_share)

    in_parts = parts_of((0, 1))
    output, input_grad = collect(out_parts, in_parts)
    grads = grads.reshape(n_mp, 3, quota, slab, BS)
    grads = lax.all_to_all(grads, MP, split_axis=0, concat_axis=0, tiled=True)
    gate_grad, up_grad, down_grad = (grads[:, p].reshape(held, slab, BS) for p in range(3))
    return (hidden_own, output, input_grad, gate_grad, up_grad, down_grad)


def solution(mesh):
    mesh = Mesh(mesh.devices.reshape(4, 2, 4, 4), DP + MP)
    wide_spec, block_spec, grad_spec = P(DP, MP), P(MP, None, None), P(MP, DP, None)
    return jax.shard_map(
        body,
        mesh=mesh,
        in_specs=(wide_spec,) * 2 + (block_spec,) * 3 + (P(),) * 4,
        out_specs=(wide_spec,) * 3 + (grad_spec,) * 3,
        check_vma=False,
    )
```

```python
import functools

import jax
import jax.numpy as jnp
from jax import lax
from jax.experimental import pallas as pl
from jax.experimental.pallas import tpu as pltpu
from jax.sharding import Mesh, PartitionSpec as P

BS = 128
UNROLL = 8
MP = ("x", "z")
DP = ("y", "c")
BF = jnp.bfloat16
F32 = jnp.float32
SMEM = pl.BlockSpec(memory_space=pltpu.SMEM)
ANY = pl.BlockSpec(memory_space=pl.ANY)
VMEM = pl.BlockSpec(memory_space=pltpu.VMEM)


def dot(a, b):
    return lax.dot_general(a, b, (((1,), (0,)), ((), ())), preferred_element_type=F32)


def dot_t(a, b):
    return lax.dot_general(a, b, (((1,), (1,)), ((), ())), preferred_element_type=F32)


def start_all(pairs, sems, first):
    copies = [pltpu.make_async_copy(a, b, sems.at[first + i]) for i, (a, b) in enumerate(pairs)]
    for copy in copies:
        copy.start()
    return copies


def wait_all(copies):
    for copy in copies:
        copy.wait()


def piece_pairs(slots, pieces, whole):
    half = whole.shape[0] // 2
    at = lambda part, i: whole.at[(part,) + (slice(None),) * (len(whole.shape) - 4) + (slots[i],)]
    own = [(pieces[i], at(slice(None), i)) for i in range(2)]
    early = [(pieces[2 * i - 2], at(slice(half), i)) for i in range(2, 8)]
    late = [(pieces[2 * i - 1], at(slice(half, 2 * half), i)) for i in range(2, 8)]
    return own, early, late


def wide(ref, block, per):
    lane = pl.multiple_of((block & (per - 1)) * BS, BS)
    return ref[block >> (per.bit_length() - 1), :, pl.ds(lane, BS)]


def each_block(low, high, rows, cols, quota, projections, visit):
    def share(i, carry):
        for proj in projections:
            for b in range(quota):
                k = (i * 3 + proj) * quota + b
                visit((i, proj, b), k, rows[k], cols[k])
        return carry

    lax.fori_loop(low, high, share, 0, unroll=UNROLL)


def send_parts(acc, stage, outs, sems, first, per, by_near):
    ring, copies = len(outs), []
    for hop in list(range(1, ring)) + [0]:
        for turn in range(ring):
            near = hop * ring + turn if by_near else turn * ring + hop
            for q in range(per):
                stage[hop, turn, :, q * BS : (q + 1) * BS] = acc[near * per + q].astype(BF)
        copies += start_all([(stage.at[hop], outs[hop])], sems, first + hop)
    return copies


def owner_kernel(rows, hops, cols, slots, x_all, *refs, ring, per, quota, owned, count):
    pieces, refs = refs[:count], refs[count:]
    act_ref, own_ref, result = refs[:3]
    outs, refs = refs[3 : 3 + ring], refs[3 + ring :]
    tok, cot, flipped, whole, acc, out_acc, flipped_hidden, stage, out_stage, sems = refs
    shares, members = whole.shape[0] // (3 * quota), tok.shape[0]
    half, line = whole.shape[0] // 2, members // 4

    def quarters(which, ref):
        return [(x_all.at[i * line : (i + 1) * line, which], ref.at[i * line : (i + 1) * line]) for i in range(4)]

    own, early, late = piece_pairs(slots, pieces, whole)
    tok_copies = start_all(quarters(0, tok), sems, 0)
    early_copies = start_all(own + early + quarters(1, cot), sems, 4)
    late_copies = start_all(late, sems, 4 + len(early_copies))
    acc[...] = jnp.zeros_like(acc)
    out_acc[...] = jnp.zeros_like(out_acc)

    index = lambda d: lax.broadcasted_iota(jnp.int32, (BS, BS), d)
    unit = jnp.where(index(0) == index(1), 1.0, 0.0).astype(BF)

    def add(at, k, r, c):
        proj, w = at[1], whole[k].reshape(BS, BS)
        if proj == 0:
            x = tok[at[0], :, at[2] * BS : (at[2] + 1) * BS]
            flipped[at[0] * per + at[2]] = x.T
        if proj < 2:
            acc[proj, c] += dot(wide(tok, r, per), w)
        else:
            acc[proj, c] += dot_t(wide(cot, r, per), w)

    wait_all(tok_copies + early_copies)
    each_block(0, shares // 2, rows, cols, quota, range(3), add)
    wait_all(late_copies)
    each_block(shares // 2, shares, rows, cols, quota, range(3), add)

    for c in range(owned):
        gate, up, grad = acc[0, c], acc[1, c], acc[2, c]
        s = jax.nn.sigmoid(gate)
        silu = gate * s
        hidden = (silu * up).astype(BF)
        act_ref[0, c] = hidden
        own_ref[:, c * BS : (c + 1) * BS] = hidden
        act_ref[1, c] = (grad * up * s * (1.0 + gate * (1.0 - s))).astype(BF)
        act_ref[2, c] = (grad * silu).astype(BF)
        flipped_hidden[c] = dot_t(unit, hidden).astype(BF)

    def down(at, k, r, c):
        out_acc[r] += dot(act_ref[0, c], whole[k].reshape(BS, BS))

    each_block(0, shares, hops, cols, quota, (2,), down)
    first = 4 + len(early_copies) + len(late_copies)
    copies = send_parts(out_acc, out_stage, outs, sems, first, per, True)

    def outer(at, k, r, c):
        if at[1] < 2:
            g = dot(flipped[r], act_ref[1 + at[1], c])
        else:
            g = dot(flipped_hidden[c], wide(cot, r, per))
        stage[:, k] = g.astype(BF).reshape(stage.shape[0], -1, BS)

    for part in range(4):
        each_block(part * shares // 4, (part + 1) * shares // 4, rows, cols, quota, range(3), outer)
        at = pl.ds(part * half // 2, half // 2)
        copies += start_all(
            [(stage.at[:, at], result.at[:, at])],
            sems,
            first + ring + part,
        )
    wait_all(copies)


def parts_kernel(rows, cols, slots, act_ref, *refs, ring, per, quota, count, projections):
    pieces, outs = refs[:count], refs[count : count + ring]
    acc, whole, stage, sems = refs[count + ring :]
    shares = whole.shape[0]
    some = slice(projections[0], projections[-1] + 1)
    own, early, late = [
        [(piece.at[:, some], place) for piece, place in pairs]
        for pairs in piece_pairs(slots, pieces, whole)
    ]
    early_copies = start_all(own + early, sems, 0)
    late_copies = start_all(late, sems, len(early_copies))
    acc[...] = jnp.zeros_like(acc)

    def add(at, k, r, c):
        w = whole[at[0], at[1] - projections[0], at[2]].reshape(BS, BS)
        if at[1] < 2:
            acc[r] += dot_t(act_ref[1 + at[1], c], w)
        else:
            acc[r] += dot(act_ref[0, c], w)

    wait_all(early_copies)
    each_block(0, shares // 2, rows, cols, quota, projections, add)
    wait_all(late_copies)
    each_block(shares // 2, shares, rows, cols, quota, projections, add)

    wait_all(send_parts(acc, stage, outs, sems, count, per, projections[0] == 2))


def shift(value, axis, hop):
    size = lax.axis_size(axis)
    return lax.ppermute(value, axis, [(i, (i + hop) % size) for i in range(size)])


def total(*terms):
    return sum(t.astype(F32) for t in terms)


def spread(mine):
    half = mine.shape[0] // 2
    parts = mine[:half], mine[half:]
    up, down = [None] * 2, [None] * 2
    up[0], down[1] = shift(parts[0], "y", 1), shift(parts[1], "y", -1)
    up[1], down[0] = shift(parts[1], "y", 1), shift(parts[0], "y", -1)
    far = [shift(up[0], "y", 1), shift(down[1], "y", -1)]
    swap = lambda value: shift(value, "c", 1)
    pieces = [mine, swap(mine)]
    for pair in (up, down, far):
        pieces += pair + [swap(v) for v in pair]
    return pieces


def collect(outs, grads):
    ring = len(outs)
    first = [[p[0]] + [shift(p[h], a, -h) for h in range(1, ring)] for p, a in ((outs, "x"), (grads, "z"))]
    done = []
    for terms, axis in zip(first, ("z", "x")):
        sums = [total(*[t[turn] for t in terms]) for turn in range(ring)]
        arrived = [shift(sums[turn].astype(BF), axis, -turn) for turn in range(1, ring)]
        done.append(total(sums[0], *arrived).astype(BF))
    return done


def body(
    tokens,
    grad_out,
    gate_weight,
    up_weight,
    down_weight,
    gate_block_pairs,
    up_blocks,
    down_blocks,
    column_order,
):
    n_mp, n_dp = lax.axis_size(MP), lax.axis_size(DP)
    member, shard = lax.axis_index(MP), lax.axis_index(DP)
    x, y, z, core = (lax.axis_index(a) for a in ("x", "y", "z", "c"))
    ring = lax.axis_size("x")
    held = gate_weight.shape[0]
    quota = held // n_mp
    slab = BS // n_dp
    per = tokens.shape[1] // BS
    n_rows = per * n_mp
    owned = column_order.shape[0] // n_mp
    count = 3 * held
    tok = tokens.shape[0]

    x_all = lax.all_gather(jnp.stack([tokens, grad_out]), MP, axis=0, tiled=False)

    slabs = jnp.stack(
        [
            lax.dynamic_slice_in_dim(w, shard * slab, slab, 1).reshape(n_mp, quota, slab, BS)
            for w in (gate_weight, up_weight, down_weight)
        ],
        axis=1,
    )
    mine = lax.all_to_all(slabs, MP, split_axis=0, concat_axis=0, tiled=True)
    weights = spread(mine.reshape(count, slab, BS))

    tables = jnp.stack([gate_block_pairs, up_blocks, down_blocks])
    tables = tables.reshape(3, n_mp, n_mp, quota, 2)
    tables = lax.dynamic_index_in_dim(tables, member, 2, keepdims=False).transpose(1, 0, 2, 3)
    is_down = (jnp.arange(3) == 2)[None, :, None]
    rows = jnp.where(is_down, tables[..., 1], tables[..., 0]).reshape(count)
    names = jnp.where(is_down, tables[..., 0], tables[..., 1]).reshape(count)
    near, far = (x + ring - rows // (per * ring)) % ring, (z + ring - rows // per % ring) % ring
    hops = (near * ring + far) * per + rows % per
    own_cols = lax.dynamic_slice_in_dim(column_order, member * owned, owned, 0)
    cols = jnp.sum(
        jnp.where(names[:, None] == own_cols[None, :], jnp.arange(owned, dtype=jnp.int32), 0),
        axis=1,
    )
    slots = jnp.stack(
        [(y + hop + ring) % ring * 2 + c for hop in (0, -1, 1, 2) for c in (core, 1 - core)]
    ).astype(jnp.int32)

    act_shape = (3, owned, tok, BS)
    x_shape = (n_mp, tok, per * BS)
    grad_shape = (n_dp, count, slab, BS)
    whole = pltpu.VMEM((count, n_dp, slab, BS), BF)
    sizes = dict(ring=ring, per=per, quota=quota, count=len(weights))

    part_shape = (ring, tok, per * BS)
    act, hidden_own, grads, *out_parts = pl.pallas_call(
        functools.partial(owner_kernel, owned=owned, **sizes),
        out_shape=[jax.ShapeDtypeStruct(act_shape, BF), jax.ShapeDtypeStruct((tok, owned * BS), BF)]
        + [jax.ShapeDtypeStruct(grad_shape, BF)]
        + [jax.ShapeDtypeStruct(part_shape, BF)] * ring,
        in_specs=[SMEM] * 4 + [ANY] * (1 + len(weights)),
        out_specs=[VMEM] * 2 + [ANY] * (1 + ring),
        scratch_shapes=[
            pltpu.VMEM(x_shape, BF),
            pltpu.VMEM(x_shape, BF),
            pltpu.VMEM((n_rows, BS, tok), BF),
            whole,
            pltpu.VMEM(act_shape, F32),
            pltpu.VMEM((n_rows, tok, BS), F32),
            pltpu.VMEM((owned, BS, tok), BF),
            pltpu.VMEM(grad_shape, BF),
            pltpu.VMEM((ring,) + part_shape, BF),
            pltpu.SemaphoreType.DMA((len(weights) + 12 + ring,)),
        ],
        name="owner",
    )(rows, hops, cols, slots, x_all, *weights)
    grads = lax.psum_scatter(grads, DP, scatter_dimension=0, tiled=True)

    by_share = [w.reshape(-1, 3, quota, slab, BS) for w in weights]

    def parts_of(projections):
        return pl.pallas_call(
            functools.partial(parts_kernel, projections=projections, **sizes),
            out_shape=[jax.ShapeDtypeStruct(part_shape, BF)] * ring,
            in_specs=[SMEM] * 3 + [VMEM] + [ANY] * len(weights),
            out_specs=[ANY] * ring,
            scratch_shapes=[
                pltpu.VMEM((n_rows, tok, BS), F32),
                pltpu.VMEM((n_mp, len(projections), quota, n_dp, slab, BS), BF),
                pltpu.VMEM((ring,) + part_shape, BF),
                pltpu.SemaphoreType.DMA((len(weights) + ring,)),
            ],
        )(hops, cols, slots, act, *by_share)

    in_parts = parts_of((0, 1))
    output, input_grad = collect(out_parts, in_parts)
    grads = grads.reshape(n_mp, 3, quota, slab, BS)
    grads = lax.all_to_all(grads, MP, split_axis=0, concat_axis=0, tiled=True)
    gate_grad, up_grad, down_grad = (grads[:, p].reshape(held, slab, BS) for p in range(3))
    return (hidden_own, output, input_grad, gate_grad, up_grad, down_grad)


def solution(mesh):
    mesh = Mesh(mesh.devices.reshape(4, 2, 4, 4), DP + MP)
    wide_spec, block_spec, grad_spec = P(DP, MP), P(MP, None, None), P(MP, DP, None)
    return jax.shard_map(
        body,
        mesh=mesh,
        in_specs=(wide_spec,) * 2 + (block_spec,) * 3 + (P(),) * 4,
        out_specs=(wide_spec,) * 3 + (grad_spec,) * 3,
        check_vma=False,
    )
```
